256 devices in a mesh: group: 16 (over z, core), blk: 16 (over y, x).
Axes of the slice: x: 4, y: 4, z: 8, core: 2. Of those that a mesh axis runs over, the one named last changes fastest.
Arguments:
- hamiltonian: bfloat16 [4096, 18, 64, 256], P(('group', 'blk')), may hold values from -0.09375 to 0.09375
- block_columns: int32 [4096, 18, 4], P(('group', 'blk')), may hold values from 0 to 15, as said below
- potential: float32 [262144], P(('group', 'blk')), may hold values from -1 to 1
- trial_slab: float32 [262144, 128], P(('group', 'blk')), may hold values from -40 to 40
Outputs:
- ortho_slab: float32 [262144, 128], P(('group', 'blk'))
- upper_factor: float32 [128, 128], replicated
The draws below stay inside these ranges and needn't reach their ends.
Inputs may be any that keep to these rules, and one draw needn't show every extreme that they name: `block_columns`: for each row block and each source, the 4 entries are distinct.
All inputs are finite; a program needn't handle non-finite values.
Results may differ from the reference program's by a relative error of at most 0.0021.
Values may be sent and summed in bfloat16 or wider, within the bound.
A program may use at most 64 MiB of HBM per device.

```python
import math
import jax
import jax.numpy as jnp
from jax import lax

BS = 64
STATES = 128
NPD = 4
RB = 16
CYCLE = 16
GROUPS = 16
NSRC = 18
ROWB = 4096
ROWS = 262144


def draw_block_columns(key, part):
    scores = jax.random.randint(key, (ROWB, NSRC, RB), 0, 1048576) * RB + jnp.arange(RB, dtype=jnp.int32)
    values, picked = lax.top_k(scores, NPD)
    return picked.astype(jnp.int32)


def draw_trial_slab(key, part):
    key_base, key_rows, key_cols = jax.random.split(jax.random.fold_in(key, 7), 3)
    row_scale = jnp.exp(jax.random.uniform(key_rows, (ROWB, 1, 1), jnp.float32, 0.0, math.log(10.0)))
    col_scale = jnp.exp(jax.random.uniform(key_cols, (1, 1, STATES), jnp.float32, 0.0, math.log(10.0)))
    base = jax.random.truncated_normal(key_base, -4.0, 4.0, (ROWB, BS, STATES), jnp.float32)
    return (0.1 * base * row_scale * col_scale).reshape(ROWS, STATES)


def steps_of(key, shape, shards, least, high):
    factor_of = 1.0
    for dim, blocks in shards:
        heights = jax.random.uniform(jax.random.fold_in(jax.random.fold_in(key, 6), dim), (blocks,), jnp.float32, least / len(shards), high / len(shards))
        factor_of = factor_of * jnp.repeat(jnp.exp(heights), shape[dim] // blocks).reshape((-1,) + (1,) * (len(shape) - 1 - dim))
    return factor_of


def scatter_about(stream_key, extent, deviation, bound, pieces=(), kind=jnp.bfloat16):
    array = deviation * jax.random.normal(stream_key, extent, jnp.float32)
    if pieces:
        array = array * steps_of(stream_key, extent, pieces, -0.22, 0.18)
    return jnp.clip(array, -bound, bound).astype(kind)


def setup_inputs(seed: int = 0) -> dict:
    splits = jax.random.split(jax.random.key(seed), 5)
    return {
        "hamiltonian": scatter_about(splits[0], (ROWB, NSRC, BS, NPD * BS), (NSRC * NPD * BS) ** -0.5, 0.09375, ((0, 256),)),
        "block_columns": draw_block_columns(jax.random.fold_in(splits[4], 71), 0),
        "potential": jnp.clip(jax.random.uniform(splits[2], (ROWS,), jnp.float32, -1.0, 1.0) * steps_of(splits[2], (ROWS,), ((0, 256),), -0.4, 0.0), -1.0, 1.0),
        "trial_slab": draw_trial_slab(jax.random.fold_in(splits[4], 71), 0),
    }


def pattern_index(block_columns):
    rows_index = jnp.arange(ROWB, dtype=jnp.int32)
    group_index = rows_index // (RB * CYCLE)
    inner_index = rows_index // RB % CYCLE
    own_base = (group_index[:, None] * CYCLE + jnp.arange(CYCLE, dtype=jnp.int32)[None, :]) * RB
    own_cols = own_base[:, :, None] + block_columns[:, :CYCLE, :]
    below_base = ((group_index - 1) * CYCLE + inner_index) * RB
    above_base = ((group_index + 1) * CYCLE + inner_index) * RB
    below_cols = jnp.where((group_index >= 1)[:, None], below_base[:, None] + block_columns[:, CYCLE, :], ROWB)
    above_cols = jnp.where((group_index < GROUPS - 1)[:, None], above_base[:, None] + block_columns[:, CYCLE + 1, :], ROWB)
    every = jnp.concatenate([own_cols, below_cols[:, None, :], above_cols[:, None, :]], axis=1)
    return every.astype(jnp.int32)

def coupled(hamiltonian, column_index, rounded):
    blocks = rounded.reshape(ROWB, BS, STATES)
    padded = jnp.concatenate([blocks, jnp.zeros((1, BS, STATES), jnp.bfloat16)], axis=0)
    ham_spans = hamiltonian.reshape(ROWB // RB, RB, NSRC, BS, NPD * BS)
    col_spans = column_index.reshape(ROWB // RB, RB, NSRC * NPD)

    def one_span(pair):
        ham_part, col_part = pair
        picked = padded[col_part].reshape(RB, NSRC, NPD * BS, STATES).astype(jnp.float32)
        return jnp.einsum('rsik,rskn->rin', ham_part.astype(jnp.float32), picked, precision=lax.Precision.HIGHEST)
    result = lax.map(one_span, (ham_spans, col_spans))
    return result.reshape(ROWS, STATES)

def reference(hamiltonian, block_columns, potential, trial_slab):
    column_index = pattern_index(block_columns)
    weights = potential[:, None]
    start_round = trial_slab.astype(jnp.bfloat16)
    filtered_once = 0.5 * (coupled(hamiltonian, column_index, start_round) + weights * trial_slab)
    once_round = filtered_once.astype(jnp.bfloat16)
    filtered = coupled(hamiltonian, column_index, once_round) + weights * filtered_once - trial_slab
    gram = jnp.dot(filtered.T, filtered, precision=lax.Precision.HIGHEST) / ROWS
    lower = jnp.linalg.cholesky(gram)
    ortho_slab = lax.linalg.triangular_solve(lower, filtered, left_side=False, lower=True, transpose_a=True)
    return (ortho_slab, jnp.transpose(lower))
```

```python
import jax
import jax.numpy as jnp
from jax import lax
from jax.sharding import PartitionSpec as P

precise = lax.Precision.HIGHEST


def neighbours(block):
    count = lax.axis_size("group")
    forward = [(i, i + 1) for i in range(count - 1)]
    backward = [(i + 1, i) for i in range(count - 1)]
    below = lax.ppermute(block, "group", forward)
    above = lax.ppermute(block, "group", backward)
    return below, above


def couple_all(hamiltonian, block_columns, rounded):
    shard_blocks, nsrc, block_size, width = hamiltonian.shape
    per_source = block_columns.shape[2]
    states = rounded.shape[2]
    gathered = lax.all_gather(rounded, "blk", axis=0, tiled=True)
    below, above = neighbours(rounded)
    table = jnp.concatenate([gathered, below, above], axis=0)
    offsets = (jnp.arange(nsrc, dtype=jnp.int32) * shard_blocks)[None, :, None]
    index = block_columns + offsets
    picked = table[index.reshape(-1)].reshape(shard_blocks, nsrc, per_source * block_size, states)
    return jnp.einsum(
        "rsik,rskn->rin", hamiltonian, picked, preferred_element_type=jnp.float32
    )


def on_device(hamiltonian, block_columns, potential, trial_slab):
    shard_blocks = hamiltonian.shape[0]
    block_size = hamiltonian.shape[2]
    states = trial_slab.shape[1]
    start_slab = trial_slab.reshape(shard_blocks, block_size, states)
    weights = potential.reshape(shard_blocks, block_size, 1)
    coupled_start = couple_all(hamiltonian, block_columns, start_slab.astype(jnp.bfloat16))
    filtered_once = 0.5 * (coupled_start + weights * start_slab)
    coupled_next = couple_all(hamiltonian, block_columns, filtered_once.astype(jnp.bfloat16))
    filtered = coupled_next + weights * filtered_once - start_slab
    flat = filtered.reshape(shard_blocks * block_size, states)
    rows_total = flat.shape[0] * lax.axis_size("group") * lax.axis_size("blk")
    local_gram = jnp.dot(flat.T, flat, precision=precise)
    gram = lax.psum(local_gram, ("group", "blk")) / rows_total
    lower = jnp.linalg.cholesky(gram)
    ortho_slab = lax.linalg.triangular_solve(
        lower, flat, left_side=False, lower=True, transpose_a=True
    )
    return (ortho_slab, jnp.transpose(lower))


def solution(mesh):
    placed = (
        P(("group", "blk"), None, None, None),
        P(("group", "blk"), None, None),
        P(("group", "blk")),
        P(("group", "blk"), None),
    )
    return jax.shard_map(
        on_device,
        mesh=mesh,
        in_specs=placed,
        out_specs=(P(("group", "blk"), None), P()),
        check_vma=False,
    )
```

```python
import jax
import jax.numpy as jnp
from jax import lax
from jax.sharding import PartitionSpec as P

precise = lax.Precision.HIGHEST


def neighbours(block):
    count = lax.axis_size("group")
    forward = [(i, i + 1) for i in range(count - 1)]
    backward = [(i + 1, i) for i in range(count - 1)]
    below = lax.ppermute(block, "group", forward)
    above = lax.ppermute(block, "group", backward)
    return below, above


def from_partner(block, axis, bit):
    count = lax.axis_size(axis)
    route = []
    for low in range(count):
        high = low | 1 << bit
        if high != low and high < count:
            route += [(low, high), (high, low)]
    return lax.ppermute(block, axis, route)


def summed_over_mesh(value):
    for axis in ("blk", "group"):
        for bit in range(lax.axis_size(axis).bit_length() - 1):
            value = value + from_partner(value, axis, bit)
    return value


def couple_all(hamiltonian, block_columns, rounded):
    shard_blocks, nsrc, block_size, width = hamiltonian.shape
    per_source = block_columns.shape[2]
    states = rounded.shape[2]
    gathered = lax.all_gather(rounded, "blk", axis=0, tiled=True)
    below, above = neighbours(rounded)
    table = jnp.concatenate([gathered, below, above], axis=0)
    offsets = (jnp.arange(nsrc, dtype=jnp.int32) * shard_blocks)[None, :, None]
    index = block_columns + offsets
    picked = table[index.reshape(-1)].reshape(shard_blocks, nsrc, per_source * block_size, states)
    return jnp.einsum(
        "rsik,rskn->rin", hamiltonian, picked, preferred_element_type=jnp.float32
    )


def on_device(hamiltonian, block_columns, potential, trial_slab):
    shard_blocks = hamiltonian.shape[0]
    block_size = hamiltonian.shape[2]
    states = trial_slab.shape[1]
    start_slab = trial_slab.reshape(shard_blocks, block_size, states)
    weights = potential.reshape(shard_blocks, block_size, 1)
    coupled_start = couple_all(hamiltonian, block_columns, start_slab.astype(jnp.bfloat16))
    filtered_once = 0.5 * (coupled_start + weights * start_slab)
    coupled_next = couple_all(hamiltonian, block_columns, filtered_once.astype(jnp.bfloat16))
    filtered = coupled_next + weights * filtered_once - start_slab
    flat = filtered.reshape(shard_blocks * block_size, states)
    rows_total = flat.shape[0] * lax.axis_size("group") * lax.axis_size("blk")
    local_gram = jnp.dot(flat.T, flat, precision=precise)
    gram = summed_over_mesh(local_gram) / rows_total
    lower = jnp.linalg.cholesky(gram)
    ortho_slab = lax.linalg.triangular_solve(
        lower, flat, left_side=False, lower=True, transpose_a=True
    )
    return (ortho_slab, jnp.transpose(lower))


def solution(mesh):
    placed = (
        P(("group", "blk"), None, None, None),
        P(("group", "blk"), None, None),
        P(("group", "blk")),
        P(("group", "blk"), None),
    )
    return jax.shard_map(
        on_device,
        mesh=mesh,
        in_specs=placed,
        out_specs=(P(("group", "blk"), None), P()),
        check_vma=False,
    )
```

```python
import functools

import jax
import jax.numpy as jnp
from jax import lax
from jax.experimental import pallas as pl
from jax.experimental.pallas import tpu as pltpu
from jax.sharding import PartitionSpec as P

precise = lax.Precision.HIGHEST
MESH = pl.DeviceIdType.MESH


def hops(t):
    ring = (0, 1, 2, 1)
    return ring[t & 3] + ring[t >> 2]


def coupling_kernel(
    cycle, groups, index_ref, own_ref, ham_hbm, out_ref, *scratch
):
    peers = cycle - 1
    held = scratch[: peers + 2]
    ham_buf, ham_sem, send_sem, recv_sem = scratch[peers + 2 :]
    shard_blocks, nsrc, block_size, width = ham_hbm.shape
    per_source = width // block_size
    me = lax.axis_index("blk")
    grp = lax.axis_index("group")
    has_below = grp > 0
    has_above = grp < groups - 1

    def remote(slot, device, dest_slot):
        return pltpu.make_async_remote_copy(
            src_ref=own_ref,
            dst_ref=held[dest_slot],
            send_sem=send_sem.at[slot],
            recv_sem=recv_sem.at[dest_slot],
            device_id=device,
            device_id_type=MESH,
        )

    barrier = pltpu.get_barrier_semaphore()
    for t in range(1, cycle):
        pl.semaphore_signal(barrier, inc=1, device_id=(grp, me ^ t), device_id_type=MESH)

    @pl.when(has_below)
    def _():
        pl.semaphore_signal(barrier, inc=1, device_id=(grp - 1, me), device_id_type=MESH)

    @pl.when(has_above)
    def _():
        pl.semaphore_signal(barrier, inc=1, device_id=(grp + 1, me), device_id_type=MESH)

    expected = peers + has_below.astype(jnp.int32) + has_above.astype(jnp.int32)
    pl.semaphore_wait(barrier, expected)

    @pl.when(has_above)
    def _():
        remote(peers, (grp + 1, me), peers).start()

    @pl.when(has_below)
    def _():
        remote(peers + 1, (grp - 1, me), peers + 1).start()

    order = sorted(range(1, cycle), key=hops)
    for t in order:
        remote(t - 1, (grp, me ^ t), t - 1).start()

    steps = [("own", 0), ("below", nsrc - 2), ("above", nsrc - 1)] + [("peer", t) for t in order]

    def source_of(kind, t):
        if kind == "own":
            return me
        if kind == "peer":
            return me ^ t
        return t

    def ham_copy(step, slot):
        kind, t = steps[step]
        return pltpu.make_async_copy(
            ham_hbm.at[:, source_of(kind, t)], ham_buf.at[slot], ham_sem.at[slot]
        )

    out_ref[...] = jnp.zeros_like(out_ref)
    ham_copy(0, 0).start()

    for step, (kind, t) in enumerate(steps):
        slot = step % 2
        if kind == "own":
            data = own_ref
        elif kind == "peer":
            data = held[t - 1]
        elif kind == "below":
            data = held[peers]
        else:
            data = held[peers + 1]
        source = source_of(kind, t)

        def work(data=data, source=source, slot=slot, step=step, kind=kind, t=t):
            if kind == "peer":
                remote(t - 1, (grp, me ^ t), t - 1).wait_recv()
            elif kind == "below":
                remote(peers, (grp, me), peers).wait_recv()
            elif kind == "above":
                remote(peers + 1, (grp, me), peers + 1).wait_recv()

            def row(r, carry):
                base = (r * nsrc + source) * per_source
                blocks = [data[index_ref[base + j]] for j in range(per_source)]
                picked = jnp.concatenate(blocks, axis=0)
                out_ref[r] += jnp.dot(
                    ham_buf[slot, r], picked, preferred_element_type=jnp.float32
                )
                return carry

            lax.fori_loop(0, shard_blocks, row, 0)

        ham_copy(step, slot).wait()
        if step + 1 < len(steps):
            ham_copy(step + 1, 1 - slot).start()
        if kind == "below":
            pl.when(has_below)(work)
        elif kind == "above":
            pl.when(has_above)(work)
        else:
            work()

    for t in order:
        remote(t - 1, (grp, me ^ t), t - 1).wait_send()

    @pl.when(has_above)
    def _():
        remote(peers, (grp + 1, me), peers).wait_send()

    @pl.when(has_below)
    def _():
        remote(peers + 1, (grp - 1, me), peers + 1).wait_send()


def couple_all(hamiltonian, index, rounded):
    shard_blocks, nsrc, block_size, width = hamiltonian.shape
    states = rounded.shape[2]
    cycle = lax.axis_size("blk")
    groups = lax.axis_size("group")
    slab = pltpu.VMEM(rounded.shape, rounded.dtype)
    flops = 2 * shard_blocks * nsrc * block_size * width * states
    return pl.pallas_call(
        functools.partial(coupling_kernel, cycle, groups),
        out_shape=jax.ShapeDtypeStruct((shard_blocks, block_size, states), jnp.float32),
        in_specs=[
            pl.BlockSpec(memory_space=pltpu.SMEM),
            pl.BlockSpec(memory_space=pltpu.VMEM),
            pl.BlockSpec(memory_space=pl.ANY),
        ],
        out_specs=pl.BlockSpec(memory_space=pltpu.VMEM),
        scratch_shapes=[slab] * (cycle + 1)
        + [
            pltpu.VMEM((2, shard_blocks, block_size, width), hamiltonian.dtype),
            pltpu.SemaphoreType.DMA((2,)),
            pltpu.SemaphoreType.DMA((cycle + 1,)),
            pltpu.SemaphoreType.DMA((cycle + 1,)),
        ],
        compiler_params=pltpu.CompilerParams(
            collective_id=0, has_side_effects=True, vmem_limit_bytes=48 * 1024 * 1024
        ),
        cost_estimate=pl.CostEstimate(
            flops=flops, transcendentals=0, bytes_accessed=hamiltonian.size * 2
        ),
    )(index, rounded, hamiltonian)


def from_partner(block, axis, bit):
    count = lax.axis_size(axis)
    route = []
    for low in range(count):
        high = low | 1 << bit
        if high != low and high < count:
            route += [(low, high), (high, low)]
    return lax.ppermute(block, axis, route)


def summed_over_mesh(value):
    for axis in ("blk", "group"):
        for bit in range(lax.axis_size(axis).bit_length() - 1):
            value = value + from_partner(value, axis, bit)
    return value


def on_device(hamiltonian, block_columns, potential, trial_slab):
    shard_blocks = hamiltonian.shape[0]
    block_size = hamiltonian.shape[2]
    states = trial_slab.shape[1]
    index = block_columns.reshape(-1)
    start_slab = trial_slab.reshape(shard_blocks, block_size, states)
    weights = potential.reshape(shard_blocks, block_size, 1)
    coupled_start = couple_all(hamiltonian, index, start_slab.astype(jnp.bfloat16))
    filtered_once = 0.5 * (coupled_start + weights * start_slab)
    coupled_next = couple_all(hamiltonian, index, filtered_once.astype(jnp.bfloat16))
    filtered = coupled_next + weights * filtered_once - start_slab
    flat = filtered.reshape(shard_blocks * block_size, states)
    rows_total = flat.shape[0] * lax.axis_size("group") * lax.axis_size("blk")
    local_gram = jnp.dot(flat.T, flat, precision=precise)
    gram = summed_over_mesh(local_gram) / rows_total
    lower = jnp.linalg.cholesky(gram)
    ortho_slab = lax.linalg.triangular_solve(
        lower, flat, left_side=False, lower=True, transpose_a=True
    )
    return (ortho_slab, jnp.transpose(lower))


def solution(mesh):
    placed = (
        P(("group", "blk"), None, None, None),
        P(("group", "blk"), None, None),
        P(("group", "blk")),
        P(("group", "blk"), None),
    )
    return jax.shard_map(
        on_device,
        mesh=mesh,
        in_specs=placed,
        out_specs=(P(("group", "blk"), None), P()),
        check_vma=False,
    )
```

```python
import functools

import jax
import jax.numpy as jnp
from jax import lax
from jax.experimental import pallas as pl
from jax.experimental.pallas import tpu as pltpu
from jax.sharding import PartitionSpec as P

precise = lax.Precision.HIGHEST
MESH = pl.DeviceIdType.MESH


def hops(t):
    ring = (0, 1, 2, 1)
    return ring[t & 3] + ring[t >> 2]


def coupling_kernel(
    cycle, groups, index_ref, own_ref, ham_hbm, out_ref, *scratch
):
    peers = cycle - 1
    held = scratch[: peers + 2]
    ham_buf, ham_sem, send_sem, recv_sem = scratch[peers + 2 :]
    shard_blocks, nsrc, block_size, width = ham_hbm.shape
    per_source = width // block_size
    me = lax.axis_index("blk")
    grp = lax.axis_index("group")
    has_below = grp > 0
    has_above = grp < groups - 1

    def remote(slot, device, dest_slot):
        return pltpu.make_async_remote_copy(
            src_ref=own_ref,
            dst_ref=held[dest_slot],
            send_sem=send_sem.at[slot],
            recv_sem=recv_sem.at[dest_slot],
            device_id=device,
            device_id_type=MESH,
        )

    barrier = pltpu.get_barrier_semaphore()
    for t in range(1, cycle):
        pl.semaphore_signal(barrier, inc=1, device_id=(grp, me ^ t), device_id_type=MESH)

    @pl.when(has_below)
    def _():
        pl.semaphore_signal(barrier, inc=1, device_id=(grp - 1, me), device_id_type=MESH)

    @pl.when(has_above)
    def _():
        pl.semaphore_signal(barrier, inc=1, device_id=(grp + 1, me), device_id_type=MESH)

    expected = peers + has_below.astype(jnp.int32) + has_above.astype(jnp.int32)
    pl.semaphore_wait(barrier, expected)

    @pl.when(has_above)
    def _():
        remote(peers, (grp + 1, me), peers).start()

    @pl.when(has_below)
    def _():
        remote(peers + 1, (grp - 1, me), peers + 1).start()

    order = sorted(range(1, cycle), key=hops)
    for t in order:
        remote(t - 1, (grp, me ^ t), t - 1).start()

    steps = [("own", 0), ("below", nsrc - 2), ("above", nsrc - 1)] + [("peer", t) for t in order]

    def source_of(kind, t):
        if kind == "own":
            return me
        if kind == "peer":
            return me ^ t
        return t

    def ham_copy(step, slot):
        kind, t = steps[step]
        return pltpu.make_async_copy(
            ham_hbm.at[:, source_of(kind, t)], ham_buf.at[slot], ham_sem.at[slot]
        )

    out_ref[...] = jnp.zeros_like(out_ref)
    ham_copy(0, 0).start()

    for step, (kind, t) in enumerate(steps):
        slot = step % 2
        if kind == "own":
            data = own_ref
        elif kind == "peer":
            data = held[t - 1]
        elif kind == "below":
            data = held[peers]
        else:
            data = held[peers + 1]
        source = source_of(kind, t)

        def work(data=data, source=source, slot=slot, step=step, kind=kind, t=t):
            if kind == "peer":
                remote(t - 1, (grp, me ^ t), t - 1).wait_recv()
            elif kind == "below":
                remote(peers, (grp, me), peers).wait_recv()
            elif kind == "above":
                remote(peers + 1, (grp, me), peers + 1).wait_recv()

            def row(r, carry):
                base = (r * nsrc + source) * per_source
                blocks = [data[index_ref[base + j]] for j in range(per_source)]
                picked = jnp.concatenate(blocks, axis=0)
                out_ref[r] += jnp.dot(
                    ham_buf[slot, r], picked, preferred_element_type=jnp.float32
                )
                return carry

            lax.fori_loop(0, shard_blocks, row, 0)

        ham_copy(step, slot).wait()
        if step + 1 < len(steps):
            ham_copy(step + 1, 1 - slot).start()
        if kind == "below":
            pl.when(has_below)(work)
        elif kind == "above":
            pl.when(has_above)(work)
        else:
            work()

    for t in order:
        remote(t - 1, (grp, me ^ t), t - 1).wait_send()

    @pl.when(has_above)
    def _():
        remote(peers, (grp + 1, me), peers).wait_send()

    @pl.when(has_below)
    def _():
        remote(peers + 1, (grp - 1, me), peers + 1).wait_send()


def couple_all(hamiltonian, index, rounded):
    shard_blocks, nsrc, block_size, width = hamiltonian.shape
    states = rounded.shape[2]
    cycle = lax.axis_size("blk")
    groups = lax.axis_size("group")
    slab = pltpu.VMEM(rounded.shape, rounded.dtype)
    flops = 2 * shard_blocks * nsrc * block_size * width * states
    return pl.pallas_call(
        functools.partial(coupling_kernel, cycle, groups),
        out_shape=jax.ShapeDtypeStruct((shard_blocks, block_size, states), jnp.float32),
        in_specs=[
            pl.BlockSpec(memory_space=pltpu.SMEM),
            pl.BlockSpec(memory_space=pltpu.VMEM),
            pl.BlockSpec(memory_space=pl.ANY),
        ],
        out_specs=pl.BlockSpec(memory_space=pltpu.VMEM),
        scratch_shapes=[slab] * (cycle + 1)
        + [
            pltpu.VMEM((2, shard_blocks, block_size, width), hamiltonian.dtype),
            pltpu.SemaphoreType.DMA((2,)),
            pltpu.SemaphoreType.DMA((cycle + 1,)),
            pltpu.SemaphoreType.DMA((cycle + 1,)),
        ],
        compiler_params=pltpu.CompilerParams(
            collective_id=0, has_side_effects=True, vmem_limit_bytes=48 * 1024 * 1024
        ),
        cost_estimate=pl.CostEstimate(
            flops=flops, transcendentals=0, bytes_accessed=hamiltonian.size * 2
        ),
    )(index, rounded, hamiltonian)


def gram_kernel(stages, gram_ref, out_ref, arrived, send_sem, recv_sem):
    place = {"group": lax.axis_index("group"), "blk": lax.axis_index("blk")}

    def partner(axis, mask):
        other = dict(place)
        other[axis] = place[axis] ^ mask
        return (other["group"], other["blk"])

    barrier = pltpu.get_barrier_semaphore()
    for axis, mask in stages:
        pl.semaphore_signal(barrier, inc=1, device_id=partner(axis, mask), device_id_type=MESH)
    pl.semaphore_wait(barrier, len(stages))
    out_ref[...] = gram_ref[...]
    for k, (axis, mask) in enumerate(stages):
        copy = pltpu.make_async_remote_copy(
            src_ref=out_ref,
            dst_ref=arrived.at[k],
            send_sem=send_sem.at[k],
            recv_sem=recv_sem.at[k],
            device_id=partner(axis, mask),
            device_id_type=MESH,
        )
        copy.start()
        copy.wait_send()
        copy.wait_recv()
        out_ref[...] = out_ref[...] + arrived[k]


def summed_over_mesh(value):
    stages = []
    for axis, masks in (("blk", (1, 3, 4, 12)), ("group", (1, 2, 4, 8))):
        size = lax.axis_size(axis)
        stages += [(axis, m) for m in masks if m < size]
    return pl.pallas_call(
        functools.partial(gram_kernel, stages),
        out_shape=jax.ShapeDtypeStruct(value.shape, value.dtype),
        in_specs=[pl.BlockSpec(memory_space=pltpu.VMEM)],
        out_specs=pl.BlockSpec(memory_space=pltpu.VMEM),
        scratch_shapes=[
            pltpu.VMEM((len(stages),) + value.shape, value.dtype),
            pltpu.SemaphoreType.DMA((len(stages),)),
            pltpu.SemaphoreType.DMA((len(stages),)),
        ],
        compiler_params=pltpu.CompilerParams(collective_id=1, has_side_effects=True),
    )(value)


def on_device(hamiltonian, block_columns, potential, trial_slab):
    shard_blocks = hamiltonian.shape[0]
    block_size = hamiltonian.shape[2]
    states = trial_slab.shape[1]
    index = block_columns.reshape(-1)
    start_slab = trial_slab.reshape(shard_blocks, block_size, states)
    weights = potential.reshape(shard_blocks, block_size, 1)
    coupled_start = couple_all(hamiltonian, index, start_slab.astype(jnp.bfloat16))
    filtered_once = 0.5 * (coupled_start + weights * start_slab)
    coupled_next = couple_all(hamiltonian, index, filtered_once.astype(jnp.bfloat16))
    filtered = coupled_next + weights * filtered_once - start_slab
    flat = filtered.reshape(shard_blocks * block_size, states)
    rows_total = flat.shape[0] * lax.axis_size("group") * lax.axis_size("blk")
    local_gram = jnp.dot(flat.T, flat, precision=precise)
    gram = summed_over_mesh(local_gram) / rows_total
    lower = jnp.linalg.cholesky(gram)
    ortho_slab = lax.linalg.triangular_solve(
        lower, flat, left_side=False, lower=True, transpose_a=True
    )
    return (ortho_slab, jnp.transpose(lower))


def solution(mesh):
    placed = (
        P(("group", "blk"), None, None, None),
        P(("group", "blk"), None, None),
        P(("group", "blk")),
        P(("group", "blk"), None),
    )
    return jax.shard_map(
        on_device,
        mesh=mesh,
        in_specs=placed,
        out_specs=(P(("group", "blk"), None), P()),
        check_vma=False,
    )
```

```python
import functools

import jax
import jax.numpy as jnp
from jax import lax
from jax.experimental import pallas as pl
from jax.experimental.pallas import tpu as pltpu
from jax.sharding import PartitionSpec as P

precise = lax.Precision.HIGHEST
MESH = pl.DeviceIdType.MESH


RING = 4
DIRECT = (1, 3, 4, 12, 2, 8)


def relayed_slots():
    both = [(ty << 2) | tx for ty in (1, 3, 2) for tx in (1, 3, 2)]
    return both


def coupling_kernel(groups, index_ref, own_ref, ham_hbm, out_ref, *scratch):
    cycle = RING * RING
    held = scratch[: cycle + 1]
    ham_buf, ham_sem, send_sem, recv_full, recv_a, recv_b, recv_side = scratch[cycle + 1 :]
    shard_blocks, nsrc, block_size, width = ham_hbm.shape
    per_source = width // block_size
    half = shard_blocks // 2
    me = lax.axis_index("blk")
    grp = lax.axis_index("group")
    has_below = grp > 0
    has_above = grp < groups - 1
    below_buf, above_buf = held[cycle - 1], held[cycle]

    def buf(t):
        return held[t - 1]

    def copy_to(src, dst, send_index, recv, device):
        return pltpu.make_async_remote_copy(
            src_ref=src,
            dst_ref=dst,
            send_sem=send_sem.at[send_index],
            recv_sem=recv,
            device_id=device,
            device_id_type=MESH,
        )

    def direct(k, t):
        return copy_to(own_ref, buf(t), k, recv_full.at[k], (grp, me ^ t))

    def relay(k, slot, peer_t, lower):
        part = pl.ds(0, half) if lower else pl.ds(half, half)
        dest = slot | peer_t
        recv = recv_a if lower else recv_b
        return copy_to(buf(slot).at[part], buf(dest).at[part], 8 + k, recv.at[dest], (grp, me ^ peer_t))

    def side(k, device):
        dst = below_buf if k == 0 else above_buf
        return copy_to(own_ref, dst, 6 + k, recv_side.at[k], device)

    barrier = pltpu.get_barrier_semaphore()
    for t in DIRECT:
        pl.semaphore_signal(barrier, inc=1, device_id=(grp, me ^ t), device_id_type=MESH)

    @pl.when(has_below)
    def _():
        pl.semaphore_signal(barrier, inc=1, device_id=(grp - 1, me), device_id_type=MESH)

    @pl.when(has_above)
    def _():
        pl.semaphore_signal(barrier, inc=1, device_id=(grp + 1, me), device_id_type=MESH)

    expected = len(DIRECT) + has_below.astype(jnp.int32) + has_above.astype(jnp.int32)
    pl.semaphore_wait(barrier, expected)

    @pl.when(has_above)
    def _():
        side(0, (grp + 1, me)).start()

    @pl.when(has_below)
    def _():
        side(1, (grp - 1, me)).start()

    for k, t in enumerate(DIRECT):
        direct(k, t).start()

    relays = []
    for k, t in enumerate(DIRECT):
        onward = (4, 12, 8) if t < RING else (1, 3, 2)
        relays.append([(len(relays) * 3 + i, t, p, t < RING) for i, p in enumerate(onward)])

    steps = [("own", 0), ("below", nsrc - 2), ("above", nsrc - 1)]
    steps += [("direct", k) for k in range(len(DIRECT))]
    steps += [("relayed", t) for t in relayed_slots()]

    def source_of(kind, t):
        if kind == "own":
            return me
        if kind == "direct":
            return me ^ DIRECT[t]
        if kind == "relayed":
            return me ^ t
        return t

    def ham_copy(step, slot):
        kind, t = steps[step]
        return pltpu.make_async_copy(
            ham_hbm.at[:, source_of(kind, t)], ham_buf.at[slot], ham_sem.at[slot]
        )

    out_ref[...] = jnp.zeros_like(out_ref)
    ham_copy(0, 0).start()

    for step, (kind, t) in enumerate(steps):
        slot = step % 2
        if kind == "own":
            data = own_ref
        elif kind == "direct":
            data = buf(DIRECT[t])
        elif kind == "relayed":
            data = buf(t)
        elif kind == "below":
            data = below_buf
        else:
            data = above_buf
        source = source_of(kind, t)

        def work(data=data, source=source, slot=slot, kind=kind, t=t):
            if kind == "direct":
                direct(t, DIRECT[t]).wait_recv()
                for k, slot_t, peer_t, lower in relays[t]:
                    relay(k, slot_t, peer_t, lower).start()
            elif kind == "relayed":
                copy_to(own_ref.at[pl.ds(0, half)], buf(t).at[pl.ds(0, half)], 0, recv_a.at[t], (grp, me)).wait_recv()
                copy_to(own_ref.at[pl.ds(half, half)], buf(t).at[pl.ds(half, half)], 0, recv_b.at[t], (grp, me)).wait_recv()
            elif kind == "below":
                side(0, (grp, me)).wait_recv()
            elif kind == "above":
                side(1, (grp, me)).wait_recv()

            def row(r, carry):
                base = (r * nsrc + source) * per_source
                blocks = [data[index_ref[base + j]] for j in range(per_source)]
                picked = jnp.concatenate(blocks, axis=0)
                out_ref[r] += jnp.dot(
                    ham_buf[slot, r], picked, preferred_element_type=jnp.float32
                )
                return carry

            lax.fori_loop(0, shard_blocks, row, 0)

        ham_copy(step, slot).wait()
        if step + 1 < len(steps):
            ham_copy(step + 1, 1 - slot).start()
        if kind == "below":
            pl.when(has_below)(work)
        elif kind == "above":
            pl.when(has_above)(work)
        else:
            work()

    for k, t in enumerate(DIRECT):
        direct(k, t).wait_send()
    for group_of in relays:
        for k, slot_t, peer_t, lower in group_of:
            relay(k, slot_t, peer_t, lower).wait_send()

    @pl.when(has_above)
    def _():
        side(0, (grp + 1, me)).wait_send()

    @pl.when(has_below)
    def _():
        side(1, (grp - 1, me)).wait_send()


def couple_all(hamiltonian, index, rounded):
    shard_blocks, nsrc, block_size, width = hamiltonian.shape
    states = rounded.shape[2]
    cycle = lax.axis_size("blk")
    assert cycle == RING * RING
    groups = lax.axis_size("group")
    slab = pltpu.VMEM(rounded.shape, rounded.dtype)
    flops = 2 * shard_blocks * nsrc * block_size * width * states
    return pl.pallas_call(
        functools.partial(coupling_kernel, groups),
        out_shape=jax.ShapeDtypeStruct((shard_blocks, block_size, states), jnp.float32),
        in_specs=[
            pl.BlockSpec(memory_space=pltpu.SMEM),
            pl.BlockSpec(memory_space=pltpu.VMEM),
            pl.BlockSpec(memory_space=pl.ANY),
        ],
        out_specs=pl.BlockSpec(memory_space=pltpu.VMEM),
        scratch_shapes=[slab] * (cycle + 1)
        + [
            pltpu.VMEM((2, shard_blocks, block_size, width), hamiltonian.dtype),
            pltpu.SemaphoreType.DMA((2,)),
            pltpu.SemaphoreType.DMA((8 + 18,)),
            pltpu.SemaphoreType.DMA((len(DIRECT),)),
            pltpu.SemaphoreType.DMA((cycle,)),
            pltpu.SemaphoreType.DMA((cycle,)),
            pltpu.SemaphoreType.DMA((2,)),
        ],
        compiler_params=pltpu.CompilerParams(
            collective_id=0, has_side_effects=True, vmem_limit_bytes=48 * 1024 * 1024
        ),
        cost_estimate=pl.CostEstimate(
            flops=flops, transcendentals=0, bytes_accessed=hamiltonian.size * 2
        ),
    )(index, rounded, hamiltonian)


def gram_kernel(stages, gram_ref, out_ref, arrived, send_sem, recv_sem):
    place = {"group": lax.axis_index("group"), "blk": lax.axis_index("blk")}

    def partner(axis, mask):
        other = dict(place)
        other[axis] = place[axis] ^ mask
        return (other["group"], other["blk"])

    barrier = pltpu.get_barrier_semaphore()
    for axis, mask in stages:
        pl.semaphore_signal(barrier, inc=1, device_id=partner(axis, mask), device_id_type=MESH)
    pl.semaphore_wait(barrier, len(stages))
    out_ref[...] = gram_ref[...]
    for k, (axis, mask) in enumerate(stages):
        copy = pltpu.make_async_remote_copy(
            src_ref=out_ref,
            dst_ref=arrived.at[k],
            send_sem=send_sem.at[k],
            recv_sem=recv_sem.at[k],
            device_id=partner(axis, mask),
            device_id_type=MESH,
        )
        copy.start()
        copy.wait_send()
        copy.wait_recv()
        out_ref[...] = out_ref[...] + arrived[k]


def summed_over_mesh(value):
    stages = []
    for axis, masks in (("blk", (1, 3, 4, 12)), ("group", (1, 2, 4, 8))):
        size = lax.axis_size(axis)
        stages += [(axis, m) for m in masks if m < size]
    return pl.pallas_call(
        functools.partial(gram_kernel, stages),
        out_shape=jax.ShapeDtypeStruct(value.shape, value.dtype),
        in_specs=[pl.BlockSpec(memory_space=pltpu.VMEM)],
        out_specs=pl.BlockSpec(memory_space=pltpu.VMEM),
        scratch_shapes=[
            pltpu.VMEM((len(stages),) + value.shape, value.dtype),
            pltpu.SemaphoreType.DMA((len(stages),)),
            pltpu.SemaphoreType.DMA((len(stages),)),
        ],
        compiler_params=pltpu.CompilerParams(collective_id=1, has_side_effects=True),
    )(value)


def on_device(hamiltonian, block_columns, potential, trial_slab):
    shard_blocks = hamiltonian.shape[0]
    block_size = hamiltonian.shape[2]
    states = trial_slab.shape[1]
    index = block_columns.reshape(-1)
    start_slab = trial_slab.reshape(shard_blocks, block_size, states)
    weights = potential.reshape(shard_blocks, block_size, 1)
    coupled_start = couple_all(hamiltonian, index, start_slab.astype(jnp.bfloat16))
    filtered_once = 0.5 * (coupled_start + weights * start_slab)
    coupled_next = couple_all(hamiltonian, index, filtered_once.astype(jnp.bfloat16))
    filtered = coupled_next + weights * filtered_once - start_slab
    flat = filtered.reshape(shard_blocks * block_size, states)
    rows_total = flat.shape[0] * lax.axis_size("group") * lax.axis_size("blk")
    local_gram = jnp.dot(flat.T, flat, precision=precise)
    gram = summed_over_mesh(local_gram) / rows_total
    lower = jnp.linalg.cholesky(gram)
    ortho_slab = lax.linalg.triangular_solve(
        lower, flat, left_side=False, lower=True, transpose_a=True
    )
    return (ortho_slab, jnp.transpose(lower))


def solution(mesh):
    placed = (
        P(("group", "blk"), None, None, None),
        P(("group", "blk"), None, None),
        P(("group", "blk")),
        P(("group", "blk"), None),
    )
    return jax.shard_map(
        on_device,
        mesh=mesh,
        in_specs=placed,
        out_specs=(P(("group", "blk"), None), P()),
        check_vma=False,
    )
```

```python
import functools

import jax
import jax.numpy as jnp
from jax import lax
from jax.experimental import pallas as pl
from jax.experimental.pallas import tpu as pltpu
from jax.sharding import PartitionSpec as P

precise = lax.Precision.HIGHEST
MESH = pl.DeviceIdType.MESH


RING = 4
DIRECT = (1, 3, 4, 12, 2, 8)


def relayed_slots():
    both = [(ty << 2) | tx for ty in (1, 3, 2) for tx in (1, 3, 2)]
    return both


def coupling_kernel(groups, index_ref, own_ref, ham_hbm, out_ref, *scratch):
    cycle = RING * RING
    held = scratch[: cycle + 1]
    ham_buf, ham_sem, send_sem, recv_full, recv_a, recv_b, recv_side = scratch[cycle + 1 :]
    shard_blocks, nsrc, block_size, width = ham_hbm.shape
    per_source = width // block_size
    half = shard_blocks // 2
    me = lax.axis_index("blk")
    grp = lax.axis_index("group")
    has_below = grp > 0
    has_above = grp < groups - 1
    below_buf, above_buf = held[cycle - 1], held[cycle]

    def buf(t):
        return held[t - 1]

    def copy_to(src, dst, send_index, recv, device):
        return pltpu.make_async_remote_copy(
            src_ref=src,
            dst_ref=dst,
            send_sem=send_sem.at[send_index],
            recv_sem=recv,
            device_id=device,
            device_id_type=MESH,
        )

    def direct(k, t):
        return copy_to(own_ref, buf(t), k, recv_full.at[k], (grp, me ^ t))

    def relay(k, slot, peer_t, lower):
        part = pl.ds(0, half) if lower else pl.ds(half, half)
        dest = slot | peer_t
        recv = recv_a if lower else recv_b
        return copy_to(buf(slot).at[part], buf(dest).at[part], 8 + k, recv.at[dest], (grp, me ^ peer_t))

    def side(k, device):
        dst = below_buf if k == 0 else above_buf
        return copy_to(own_ref, dst, 6 + k, recv_side.at[k], device)

    barrier = pltpu.get_barrier_semaphore()
    for t in DIRECT:
        pl.semaphore_signal(barrier, inc=1, device_id=(grp, me ^ t), device_id_type=MESH)

    @pl.when(has_below)
    def _():
        pl.semaphore_signal(barrier, inc=1, device_id=(grp - 1, me), device_id_type=MESH)

    @pl.when(has_above)
    def _():
        pl.semaphore_signal(barrier, inc=1, device_id=(grp + 1, me), device_id_type=MESH)

    expected = len(DIRECT) + has_below.astype(jnp.int32) + has_above.astype(jnp.int32)
    pl.semaphore_wait(barrier, expected)

    @pl.when(has_above)
    def _():
        side(0, (grp + 1, me)).start()

    @pl.when(has_below)
    def _():
        side(1, (grp - 1, me)).start()

    for k, t in enumerate(DIRECT):
        direct(k, t).start()

    relays = []
    for k, t in enumerate(DIRECT):
        onward = (4, 12, 8) if t < RING else (1, 3, 2)
        relays.append([(len(relays) * 3 + i, t, p, t < RING) for i, p in enumerate(onward)])

    steps = [("own", 0), ("below", nsrc - 2), ("above", nsrc - 1)]
    steps += [("direct", k) for k in range(len(DIRECT))]
    steps += [("relayed", t) for t in relayed_slots()]

    def source_of(kind, t):
        if kind == "own":
            return me
        if kind == "direct":
            return me ^ DIRECT[t]
        if kind == "relayed":
            return me ^ t
        return t

    def ham_copy(step, slot):
        kind, t = steps[step]
        return pltpu.make_async_copy(
            ham_hbm.at[:, source_of(kind, t)], ham_buf.at[slot], ham_sem.at[slot]
        )

    out_ref[...] = jnp.zeros_like(out_ref)
    ham_copy(0, 0).start()

    for step, (kind, t) in enumerate(steps):
        slot = step % 2
        if kind == "own":
            data = own_ref
        elif kind == "direct":
            data = buf(DIRECT[t])
        elif kind == "relayed":
            data = buf(t)
        elif kind == "below":
            data = below_buf
        else:
            data = above_buf
        source = source_of(kind, t)

        def work(data=data, source=source, slot=slot, kind=kind, t=t):
            if kind == "direct":
                direct(t, DIRECT[t]).wait_recv()
                for k, slot_t, peer_t, lower in relays[t]:
                    relay(k, slot_t, peer_t, lower).start()
            elif kind == "relayed":
                copy_to(own_ref.at[pl.ds(0, half)], buf(t).at[pl.ds(0, half)], 0, recv_a.at[t], (grp, me)).wait_recv()
                copy_to(own_ref.at[pl.ds(half, half)], buf(t).at[pl.ds(half, half)], 0, recv_b.at[t], (grp, me)).wait_recv()
            elif kind == "below":
                side(0, (grp, me)).wait_recv()
            elif kind == "above":
                side(1, (grp, me)).wait_recv()

            def row(r, carry):
                base = (r * nsrc + source) * per_source
                blocks = [data[index_ref[base + j]] for j in range(per_source)]
                picked = jnp.concatenate(blocks, axis=0)
                out_ref[r] += jnp.dot(
                    ham_buf[slot, r], picked, preferred_element_type=jnp.float32
                )
                return carry

            lax.fori_loop(0, shard_blocks, row, 0, unroll=True)

        ham_copy(step, slot).wait()
        if step + 1 < len(steps):
            ham_copy(step + 1, 1 - slot).start()
        if kind == "below":
            pl.when(has_below)(work)
        elif kind == "above":
            pl.when(has_above)(work)
        else:
            work()

    for k, t in enumerate(DIRECT):
        direct(k, t).wait_send()
    for group_of in relays:
        for k, slot_t, peer_t, lower in group_of:
            relay(k, slot_t, peer_t, lower).wait_send()

    @pl.when(has_above)
    def _():
        side(0, (grp + 1, me)).wait_send()

    @pl.when(has_below)
    def _():
        side(1, (grp - 1, me)).wait_send()


def couple_all(hamiltonian, index, rounded):
    shard_blocks, nsrc, block_size, width = hamiltonian.shape
    states = rounded.shape[2]
    cycle = lax.axis_size("blk")
    assert cycle == RING * RING
    groups = lax.axis_size("group")
    slab = pltpu.VMEM(rounded.shape, rounded.dtype)
    flops = 2 * shard_blocks * nsrc * block_size * width * states
    return pl.pallas_call(
        functools.partial(coupling_kernel, groups),
        out_shape=jax.ShapeDtypeStruct((shard_blocks, block_size, states), jnp.float32),
        in_specs=[
            pl.BlockSpec(memory_space=pltpu.SMEM),
            pl.BlockSpec(memory_space=pltpu.VMEM),
            pl.BlockSpec(memory_space=pl.ANY),
        ],
        out_specs=pl.BlockSpec(memory_space=pltpu.VMEM),
        scratch_shapes=[slab] * (cycle + 1)
        + [
            pltpu.VMEM((2, shard_blocks, block_size, width), hamiltonian.dtype),
            pltpu.SemaphoreType.DMA((2,)),
            pltpu.SemaphoreType.DMA((8 + 18,)),
            pltpu.SemaphoreType.DMA((len(DIRECT),)),
            pltpu.SemaphoreType.DMA((cycle,)),
            pltpu.SemaphoreType.DMA((cycle,)),
            pltpu.SemaphoreType.DMA((2,)),
        ],
        compiler_params=pltpu.CompilerParams(
            collective_id=0, has_side_effects=True, vmem_limit_bytes=48 * 1024 * 1024
        ),
        cost_estimate=pl.CostEstimate(
            flops=flops, transcendentals=0, bytes_accessed=hamiltonian.size * 2
        ),
    )(index, rounded, hamiltonian)


def gram_kernel(stages, gram_ref, out_ref, arrived, send_sem, recv_sem):
    place = {"group": lax.axis_index("group"), "blk": lax.axis_index("blk")}

    def partner(axis, mask):
        other = dict(place)
        other[axis] = place[axis] ^ mask
        return (other["group"], other["blk"])

    barrier = pltpu.get_barrier_semaphore()
    for axis, mask in stages:
        pl.semaphore_signal(barrier, inc=1, device_id=partner(axis, mask), device_id_type=MESH)
    pl.semaphore_wait(barrier, len(stages))
    out_ref[...] = gram_ref[...]
    for k, (axis, mask) in enumerate(stages):
        copy = pltpu.make_async_remote_copy(
            src_ref=out_ref,
            dst_ref=arrived.at[k],
            send_sem=send_sem.at[k],
            recv_sem=recv_sem.at[k],
            device_id=partner(axis, mask),
            device_id_type=MESH,
        )
        copy.start()
        copy.wait_send()
        copy.wait_recv()
        out_ref[...] = out_ref[...] + arrived[k]


def summed_over_mesh(value):
    stages = []
    for axis, masks in (("blk", (1, 3, 4, 12)), ("group", (1, 2, 4, 8))):
        size = lax.axis_size(axis)
        stages += [(axis, m) for m in masks if m < size]
    return pl.pallas_call(
        functools.partial(gram_kernel, stages),
        out_shape=jax.ShapeDtypeStruct(value.shape, value.dtype),
        in_specs=[pl.BlockSpec(memory_space=pltpu.VMEM)],
        out_specs=pl.BlockSpec(memory_space=pltpu.VMEM),
        scratch_shapes=[
            pltpu.VMEM((len(stages),) + value.shape, value.dtype),
            pltpu.SemaphoreType.DMA((len(stages),)),
            pltpu.SemaphoreType.DMA((len(stages),)),
        ],
        compiler_params=pltpu.CompilerParams(collective_id=1, has_side_effects=True),
    )(value)


def on_device(hamiltonian, block_columns, potential, trial_slab):
    shard_blocks = hamiltonian.shape[0]
    block_size = hamiltonian.shape[2]
    states = trial_slab.shape[1]
    index = block_columns.reshape(-1)
    start_slab = trial_slab.reshape(shard_blocks, block_size, states)
    weights = potential.reshape(shard_blocks, block_size, 1)
    coupled_start = couple_all(hamiltonian, index, start_slab.astype(jnp.bfloat16))
    filtered_once = 0.5 * (coupled_start + weights * start_slab)
    coupled_next = couple_all(hamiltonian, index, filtered_once.astype(jnp.bfloat16))
    filtered = coupled_next + weights * filtered_once - start_slab
    flat = filtered.reshape(shard_blocks * block_size, states)
    rows_total = flat.shape[0] * lax.axis_size("group") * lax.axis_size("blk")
    local_gram = jnp.dot(flat.T, flat, precision=precise)
    gram = summed_over_mesh(local_gram) / rows_total
    lower = jnp.linalg.cholesky(gram)
    ortho_slab = lax.linalg.triangular_solve(
        lower, flat, left_side=False, lower=True, transpose_a=True
    )
    return (ortho_slab, jnp.transpose(lower))


def solution(mesh):
    placed = (
        P(("group", "blk"), None, None, None),
        P(("group", "blk"), None, None),
        P(("group", "blk")),
        P(("group", "blk"), None),
    )
    return jax.shard_map(
        on_device,
        mesh=mesh,
        in_specs=placed,
        out_specs=(P(("group", "blk"), None), P()),
        check_vma=False,
    )
```

```python
import functools

import jax
import jax.numpy as jnp
from jax import lax
from jax.experimental import pallas as pl
from jax.experimental.pallas import tpu as pltpu
from jax.sharding import PartitionSpec as P

precise = lax.Precision.HIGHEST
MESH = pl.DeviceIdType.MESH


RING = 4
DIRECT = (1, 3, 4, 12, 2, 8)


def relayed_slots():
    both = [(ty << 2) | tx for ty in (1, 3, 2) for tx in (1, 3, 2)]
    return both


def coupling_kernel(groups, index_ref, own_ref, ham_hbm, out_ref, *scratch):
    cycle = RING * RING
    held = scratch[: cycle + 1]
    ham_buf, ham_sem, send_sem, recv_full, recv_a, recv_b, recv_side = scratch[cycle + 1 :]
    shard_blocks, nsrc, block_size, width = ham_hbm.shape
    per_source = width // block_size
    half = shard_blocks // 2
    me = lax.axis_index("blk")
    grp = lax.axis_index("group")
    has_below = grp > 0
    has_above = grp < groups - 1
    below_buf, above_buf = held[cycle - 1], held[cycle]

    def buf(t):
        return held[t - 1]

    def copy_to(src, dst, send_index, recv, device):
        return pltpu.make_async_remote_copy(
            src_ref=src,
            dst_ref=dst,
            send_sem=send_sem.at[send_index],
            recv_sem=recv,
            device_id=device,
            device_id_type=MESH,
        )

    def direct(k, t):
        return copy_to(own_ref, buf(t), k, recv_full.at[k], (grp, me ^ t))

    def relay(k, slot, peer_t, lower):
        part = pl.ds(0, half) if lower else pl.ds(half, half)
        dest = slot | peer_t
        recv = recv_a if lower else recv_b
        return copy_to(buf(slot).at[part], buf(dest).at[part], 8 + k, recv.at[dest], (grp, me ^ peer_t))

    def side(k, device):
        dst = below_buf if k == 0 else above_buf
        return copy_to(own_ref, dst, 6 + k, recv_side.at[k], device)

    barrier = pltpu.get_barrier_semaphore()
    for t in DIRECT:
        pl.semaphore_signal(barrier, inc=1, device_id=(grp, me ^ t), device_id_type=MESH)

    @pl.when(has_below)
    def _():
        pl.semaphore_signal(barrier, inc=1, device_id=(grp - 1, me), device_id_type=MESH)

    @pl.when(has_above)
    def _():
        pl.semaphore_signal(barrier, inc=1, device_id=(grp + 1, me), device_id_type=MESH)

    expected = len(DIRECT) + has_below.astype(jnp.int32) + has_above.astype(jnp.int32)
    pl.semaphore_wait(barrier, expected)

    @pl.when(has_above)
    def _():
        side(0, (grp + 1, me)).start()

    @pl.when(has_below)
    def _():
        side(1, (grp - 1, me)).start()

    for k, t in enumerate(DIRECT):
        direct(k, t).start()

    relays = []
    for k, t in enumerate(DIRECT):
        onward = (4, 12, 8) if t < RING else (1, 3, 2)
        relays.append([(len(relays) * 3 + i, t, p, t < RING) for i, p in enumerate(onward)])

    steps = [("own", 0), ("below", nsrc - 2), ("above", nsrc - 1)]
    steps += [("direct", k) for k in range(len(DIRECT))]
    steps += [("relayed", t) for t in relayed_slots()]

    def source_of(kind, t):
        if kind == "own":
            return me
        if kind == "direct":
            return me ^ DIRECT[t]
        if kind == "relayed":
            return me ^ t
        return t

    def ham_copy(step, slot):
        kind, t = steps[step]
        return pltpu.make_async_copy(
            ham_hbm.at[:, source_of(kind, t)], ham_buf.at[slot], ham_sem.at[slot]
        )

    out_ref[...] = jnp.zeros_like(out_ref)
    ham_copy(0, 0).start()

    for step, (kind, t) in enumerate(steps):
        slot = step % 2
        if kind == "own":
            data = own_ref
        elif kind == "direct":
            data = buf(DIRECT[t])
        elif kind == "relayed":
            data = buf(t)
        elif kind == "below":
            data = below_buf
        else:
            data = above_buf
        source = source_of(kind, t)

        def work(data=data, source=source, slot=slot, kind=kind, t=t):
            if kind == "direct":
                direct(t, DIRECT[t]).wait_recv()
                for k, slot_t, peer_t, lower in relays[t]:
                    relay(k, slot_t, peer_t, lower).start()
            elif kind == "relayed":
                copy_to(own_ref.at[pl.ds(0, half)], buf(t).at[pl.ds(0, half)], 0, recv_a.at[t], (grp, me)).wait_recv()
                copy_to(own_ref.at[pl.ds(half, half)], buf(t).at[pl.ds(half, half)], 0, recv_b.at[t], (grp, me)).wait_recv()
            elif kind == "below":
                side(0, (grp, me)).wait_recv()
            elif kind == "above":
                side(1, (grp, me)).wait_recv()

            def row(r, carry):
                base = (r * nsrc + source) * per_source
                blocks = [data[index_ref[base + j]] for j in range(per_source)]
                picked = jnp.concatenate(blocks, axis=0)
                out_ref[r] += jnp.dot(
                    ham_buf[slot, r], picked, preferred_element_type=jnp.float32
                )
                return carry

            lax.fori_loop(0, shard_blocks, row, 0, unroll=True)

        ham_copy(step, slot).wait()
        if step + 1 < len(steps):
            ham_copy(step + 1, 1 - slot).start()
        if kind == "below":
            pl.when(has_below)(work)
        elif kind == "above":
            pl.when(has_above)(work)
        else:
            work()

    for k, t in enumerate(DIRECT):
        direct(k, t).wait_send()
    for group_of in relays:
        for k, slot_t, peer_t, lower in group_of:
            relay(k, slot_t, peer_t, lower).wait_send()

    @pl.when(has_above)
    def _():
        side(0, (grp + 1, me)).wait_send()

    @pl.when(has_below)
    def _():
        side(1, (grp - 1, me)).wait_send()


def couple_all(hamiltonian, index, rounded):
    shard_blocks, nsrc, block_size, width = hamiltonian.shape
    states = rounded.shape[2]
    cycle = lax.axis_size("blk")
    assert cycle == RING * RING
    groups = lax.axis_size("group")
    slab = pltpu.VMEM(rounded.shape, rounded.dtype)
    flops = 2 * shard_blocks * nsrc * block_size * width * states
    return pl.pallas_call(
        functools.partial(coupling_kernel, groups),
        out_shape=jax.ShapeDtypeStruct((shard_blocks, block_size, states), jnp.float32),
        in_specs=[
            pl.BlockSpec(memory_space=pltpu.SMEM),
            pl.BlockSpec(memory_space=pltpu.VMEM),
            pl.BlockSpec(memory_space=pl.ANY),
        ],
        out_specs=pl.BlockSpec(memory_space=pltpu.VMEM),
        scratch_shapes=[slab] * (cycle + 1)
        + [
            pltpu.VMEM((2, shard_blocks, block_size, width), hamiltonian.dtype),
            pltpu.SemaphoreType.DMA((2,)),
            pltpu.SemaphoreType.DMA((8 + 18,)),
            pltpu.SemaphoreType.DMA((len(DIRECT),)),
            pltpu.SemaphoreType.DMA((cycle,)),
            pltpu.SemaphoreType.DMA((cycle,)),
            pltpu.SemaphoreType.DMA((2,)),
        ],
        compiler_params=pltpu.CompilerParams(
            collective_id=0, has_side_effects=True, vmem_limit_bytes=48 * 1024 * 1024
        ),
        cost_estimate=pl.CostEstimate(
            flops=flops, transcendentals=0, bytes_accessed=hamiltonian.size * 2
        ),
    )(index, rounded, hamiltonian)


def gram_kernel(stages, gram_ref, out_ref, arrived, send_sem, recv_sem):
    place = {"group": lax.axis_index("group"), "blk": lax.axis_index("blk")}
    members = 4

    def field(axis, shift):
        return (place[axis] >> shift) % members

    def peer(axis, shift, position):
        other = dict(place)
        other[axis] = place[axis] + (position - field(axis, shift)) * (1 << shift)
        return (other["group"], other["blk"])

    barrier = pltpu.get_barrier_semaphore()
    for axis, shift in stages:
        for m in range(1, members):
            pl.semaphore_signal(
                barrier, inc=1, device_id=peer(axis, shift, field(axis, shift) ^ m), device_id_type=MESH
            )
    pl.semaphore_wait(barrier, len(stages) * (members - 1))
    out_ref[...] = gram_ref[...]
    for k, (axis, shift) in enumerate(stages):
        mine = field(axis, shift)

        def exchange(position, m):
            return pltpu.make_async_remote_copy(
                src_ref=out_ref,
                dst_ref=arrived.at[k, mine],
                send_sem=send_sem.at[k, m],
                recv_sem=recv_sem.at[k, mine],
                device_id=peer(axis, shift, position),
                device_id_type=MESH,
            )

        def incoming(position):
            return pltpu.make_async_remote_copy(
                src_ref=out_ref,
                dst_ref=arrived.at[k, position],
                send_sem=send_sem.at[k, 0],
                recv_sem=recv_sem.at[k, position],
                device_id=peer(axis, shift, position),
                device_id_type=MESH,
            )

        for m in range(1, members):
            exchange(mine ^ m, m).start()
        arrived[k, mine] = out_ref[...]
        for m in range(1, members):
            exchange(mine ^ m, m).wait_send()
        for m in range(1, members):
            incoming(mine ^ m).wait_recv()
        total = arrived[k, 0]
        for position in range(1, members):
            total = total + arrived[k, position]
        out_ref[...] = total


def summed_over_mesh(value):
    stages = []
    for axis in ("blk", "group"):
        size = lax.axis_size(axis)
        assert size == 16
        stages += [(axis, 0), (axis, 2)]
    return pl.pallas_call(
        functools.partial(gram_kernel, stages),
        out_shape=jax.ShapeDtypeStruct(value.shape, value.dtype),
        in_specs=[pl.BlockSpec(memory_space=pltpu.VMEM)],
        out_specs=pl.BlockSpec(memory_space=pltpu.VMEM),
        scratch_shapes=[
            pltpu.VMEM((len(stages), 4) + value.shape, value.dtype),
            pltpu.SemaphoreType.DMA((len(stages), 4)),
            pltpu.SemaphoreType.DMA((len(stages), 4)),
        ],
        compiler_params=pltpu.CompilerParams(collective_id=1, has_side_effects=True),
    )(value)


def on_device(hamiltonian, block_columns, potential, trial_slab):
    shard_blocks = hamiltonian.shape[0]
    block_size = hamiltonian.shape[2]
    states = trial_slab.shape[1]
    index = block_columns.reshape(-1)
    start_slab = trial_slab.reshape(shard_blocks, block_size, states)
    weights = potential.reshape(shard_blocks, block_size, 1)
    coupled_start = couple_all(hamiltonian, index, start_slab.astype(jnp.bfloat16))
    filtered_once = 0.5 * (coupled_start + weights * start_slab)
    coupled_next = couple_all(hamiltonian, index, filtered_once.astype(jnp.bfloat16))
    filtered = coupled_next + weights * filtered_once - start_slab
    flat = filtered.reshape(shard_blocks * block_size, states)
    rows_total = flat.shape[0] * lax.axis_size("group") * lax.axis_size("blk")
    local_gram = jnp.dot(flat.T, flat, precision=precise)
    gram = summed_over_mesh(local_gram) / rows_total
    lower = jnp.linalg.cholesky(gram)
    ortho_slab = lax.linalg.triangular_solve(
        lower, flat, left_side=False, lower=True, transpose_a=True
    )
    return (ortho_slab, jnp.transpose(lower))


def solution(mesh):
    placed = (
        P(("group", "blk"), None, None, None),
        P(("group", "blk"), None, None),
        P(("group", "blk")),
        P(("group", "blk"), None),
    )
    return jax.shard_map(
        on_device,
        mesh=mesh,
        in_specs=placed,
        out_specs=(P(("group", "blk"), None), P()),
        check_vma=False,
    )
```

```python
import functools

import jax
import jax.numpy as jnp
from jax import lax
from jax.experimental import pallas as pl
from jax.experimental.pallas import tpu as pltpu
from jax.sharding import PartitionSpec as P

precise = lax.Precision.HIGHEST
MESH = pl.DeviceIdType.MESH


RING = 4
QUARTERS = 4
NEIGHBOURS = (1, 3, 4, 12)


def forwards(t, q):
    tx, ty = t & 3, t >> 2
    out = []
    if q < 2:
        if t == 0:
            out += [1, 3]
        if ty == 0 and tx == 1 and q == 0:
            out.append(3)
        if ty == 0 and tx == 3 and q == 1:
            out.append(1)
        if ty == 0:
            out += [4, 12]
        if ty == 1 and q == 0:
            out.append(12)
        if ty == 3 and q == 1:
            out.append(4)
    else:
        if t == 0:
            out += [4, 12]
        if tx == 0 and ty == 1 and q == 2:
            out.append(12)
        if tx == 0 and ty == 3 and q == 3:
            out.append(4)
        if tx == 0:
            out += [1, 3]
        if tx == 1 and q == 2:
            out.append(3)
        if tx == 3 and q == 3:
            out.append(1)
    return out


def schedule():
    level = {(0, q): 0 for q in range(QUARTERS)}
    sends = []
    frontier = [(0, q) for q in range(QUARTERS)]
    while frontier:
        nxt = []
        for t, q in frontier:
            for d in forwards(t, q):
                dest = (t ^ d, q)
                assert dest not in level
                level[dest] = level[(t, q)] + 1
                sends.append((t, q, d))
                nxt.append(dest)
        frontier = nxt
    assert len(level) == RING * RING * QUARTERS
    return level, sends


def coupling_kernel(groups, index_ref, own_ref, ham_hbm, out_ref, *scratch):
    cycle = RING * RING
    held = scratch[: cycle + 1]
    ham_buf, ham_sem, send_sem, recv_sem, side_send, side_recv = scratch[cycle + 1 :]
    shard_blocks, nsrc, block_size, width = ham_hbm.shape
    per_source = width // block_size
    part = shard_blocks // QUARTERS
    me = lax.axis_index("blk")
    grp = lax.axis_index("group")
    has_below = grp > 0
    has_above = grp < groups - 1
    below_buf, above_buf = held[cycle - 1], held[cycle]
    level, sends = schedule()
    send_index = {item: k for k, item in enumerate(sends)}

    def buf(t):
        return own_ref if t == 0 else held[t - 1]

    def quarter(ref, q):
        return ref.at[pl.ds(q * part, part)]

    def link(t, q, d):
        return pltpu.make_async_remote_copy(
            src_ref=quarter(buf(t), q),
            dst_ref=quarter(buf(t ^ d), q),
            send_sem=send_sem.at[send_index[(t, q, d)]],
            recv_sem=recv_sem.at[t ^ d, q],
            device_id=(grp, me ^ d),
            device_id_type=MESH,
        )

    def arrival(t, q):
        return pltpu.make_async_remote_copy(
            src_ref=quarter(own_ref, q),
            dst_ref=quarter(buf(t), q),
            send_sem=side_send.at[0],
            recv_sem=recv_sem.at[t, q],
            device_id=(grp, me),
            device_id_type=MESH,
        )

    def side(k, device):
        dst = below_buf if k == 0 else above_buf
        return pltpu.make_async_remote_copy(
            src_ref=own_ref,
            dst_ref=dst,
            send_sem=side_send.at[k],
            recv_sem=side_recv.at[k],
            device_id=device,
            device_id_type=MESH,
        )

    barrier = pltpu.get_barrier_semaphore()
    for d in NEIGHBOURS:
        pl.semaphore_signal(barrier, inc=1, device_id=(grp, me ^ d), device_id_type=MESH)

    @pl.when(has_below)
    def _():
        pl.semaphore_signal(barrier, inc=1, device_id=(grp - 1, me), device_id_type=MESH)

    @pl.when(has_above)
    def _():
        pl.semaphore_signal(barrier, inc=1, device_id=(grp + 1, me), device_id_type=MESH)

    expected = len(NEIGHBOURS) + has_below.astype(jnp.int32) + has_above.astype(jnp.int32)
    pl.semaphore_wait(barrier, expected)

    for t, q, d in sends:
        if t == 0:
            link(t, q, d).start()

    @pl.when(has_above)
    def _():
        side(0, (grp + 1, me)).start()

    @pl.when(has_below)
    def _():
        side(1, (grp - 1, me)).start()

    top = max(level.values())
    steps = [("own", 0), ("below", nsrc - 2), ("above", nsrc - 1)]
    for lv in range(1, top + 1):
        ready = [t for t in range(1, cycle) if max(level[(t, q)] for q in range(QUARTERS)) == lv]
        steps.append(("arrive", lv))
        steps += [("slot", t) for t in ready]

    compute_steps = [s for s in steps if s[0] != "arrive"]

    def source_of(kind, t):
        if kind == "own":
            return me
        if kind == "slot":
            return me ^ t
        return t

    def ham_copy(i, slot):
        kind, t = compute_steps[i]
        return pltpu.make_async_copy(
            ham_hbm.at[:, source_of(kind, t)], ham_buf.at[slot], ham_sem.at[slot]
        )

    out_ref[...] = jnp.zeros_like(out_ref)
    ham_copy(0, 0).start()

    i = 0
    for kind, t in steps:
        if kind == "arrive":
            for (slot_t, q), v in sorted(level.items()):
                if v == t:
                    arrival(slot_t, q).wait_recv()
                    for d in forwards(slot_t, q):
                        link(slot_t, q, d).start()
            continue
        slot = i % 2
        if kind == "own":
            data = own_ref
        elif kind == "slot":
            data = buf(t)
        elif kind == "below":
            data = below_buf
        else:
            data = above_buf
        source = source_of(kind, t)

        def work(data=data, source=source, slot=slot, kind=kind):
            if kind == "below":
                side(0, (grp, me)).wait_recv()
            elif kind == "above":
                side(1, (grp, me)).wait_recv()

            def row(r, carry):
                base = (r * nsrc + source) * per_source
                blocks = [data[index_ref[base + j]] for j in range(per_source)]
                picked = jnp.concatenate(blocks, axis=0)
                out_ref[r] += jnp.dot(
                    ham_buf[slot, r], picked, preferred_element_type=jnp.float32
                )
                return carry

            lax.fori_loop(0, shard_blocks, row, 0, unroll=True)

        ham_copy(i, slot).wait()
        if i + 1 < len(compute_steps):
            ham_copy(i + 1, 1 - slot).start()
        if kind == "below":
            pl.when(has_below)(work)
        elif kind == "above":
            pl.when(has_above)(work)
        else:
            work()
        i += 1

    for t, q, d in sends:
        link(t, q, d).wait_send()

    @pl.when(has_above)
    def _():
        side(0, (grp + 1, me)).wait_send()

    @pl.when(has_below)
    def _():
        side(1, (grp - 1, me)).wait_send()


def couple_all(hamiltonian, index, rounded):
    shard_blocks, nsrc, block_size, width = hamiltonian.shape
    states = rounded.shape[2]
    cycle = lax.axis_size("blk")
    assert cycle == RING * RING
    groups = lax.axis_size("group")
    slab = pltpu.VMEM(rounded.shape, rounded.dtype)
    flops = 2 * shard_blocks * nsrc * block_size * width * states
    return pl.pallas_call(
        functools.partial(coupling_kernel, groups),
        out_shape=jax.ShapeDtypeStruct((shard_blocks, block_size, states), jnp.float32),
        in_specs=[
            pl.BlockSpec(memory_space=pltpu.SMEM),
            pl.BlockSpec(memory_space=pltpu.VMEM),
            pl.BlockSpec(memory_space=pl.ANY),
        ],
        out_specs=pl.BlockSpec(memory_space=pltpu.VMEM),
        scratch_shapes=[slab] * (cycle + 1)
        + [
            pltpu.VMEM((2, shard_blocks, block_size, width), hamiltonian.dtype),
            pltpu.SemaphoreType.DMA((2,)),
            pltpu.SemaphoreType.DMA((len(schedule()[1]),)),
            pltpu.SemaphoreType.DMA((cycle, QUARTERS)),
            pltpu.SemaphoreType.DMA((2,)),
            pltpu.SemaphoreType.DMA((2,)),
        ],
        compiler_params=pltpu.CompilerParams(
            collective_id=0, has_side_effects=True, vmem_limit_bytes=48 * 1024 * 1024
        ),
        cost_estimate=pl.CostEstimate(
            flops=flops, transcendentals=0, bytes_accessed=hamiltonian.size * 2
        ),
    )(index, rounded, hamiltonian)


def gram_kernel(stages, gram_ref, out_ref, arrived, send_sem, recv_sem):
    place = {"group": lax.axis_index("group"), "blk": lax.axis_index("blk")}
    members = 4

    def field(axis, shift):
        return (place[axis] >> shift) % members

    def peer(axis, shift, position):
        other = dict(place)
        other[axis] = place[axis] + (position - field(axis, shift)) * (1 << shift)
        return (other["group"], other["blk"])

    barrier = pltpu.get_barrier_semaphore()
    for axis, shift in stages:
        for m in range(1, members):
            pl.semaphore_signal(
                barrier, inc=1, device_id=peer(axis, shift, field(axis, shift) ^ m), device_id_type=MESH
            )
    pl.semaphore_wait(barrier, len(stages) * (members - 1))
    out_ref[...] = gram_ref[...]
    for k, (axis, shift) in enumerate(stages):
        mine = field(axis, shift)

        def exchange(position, m):
            return pltpu.make_async_remote_copy(
                src_ref=out_ref,
                dst_ref=arrived.at[k, mine],
                send_sem=send_sem.at[k, m],
                recv_sem=recv_sem.at[k, mine],
                device_id=peer(axis, shift, position),
                device_id_type=MESH,
            )

        def incoming(position):
            return pltpu.make_async_remote_copy(
                src_ref=out_ref,
                dst_ref=arrived.at[k, position],
                send_sem=send_sem.at[k, 0],
                recv_sem=recv_sem.at[k, position],
                device_id=peer(axis, shift, position),
                device_id_type=MESH,
            )

        for m in range(1, members):
            exchange(mine ^ m, m).start()
        arrived[k, mine] = out_ref[...]
        for m in range(1, members):
            exchange(mine ^ m, m).wait_send()
        for m in range(1, members):
            incoming(mine ^ m).wait_recv()
        total = arrived[k, 0]
        for position in range(1, members):
            total = total + arrived[k, position]
        out_ref[...] = total


def summed_over_mesh(value):
    stages = []
    for axis in ("blk", "group"):
        size = lax.axis_size(axis)
        assert size == 16
        stages += [(axis, 0), (axis, 2)]
    return pl.pallas_call(
        functools.partial(gram_kernel, stages),
        out_shape=jax.ShapeDtypeStruct(value.shape, value.dtype),
        in_specs=[pl.BlockSpec(memory_space=pltpu.VMEM)],
        out_specs=pl.BlockSpec(memory_space=pltpu.VMEM),
        scratch_shapes=[
            pltpu.VMEM((len(stages), 4) + value.shape, value.dtype),
            pltpu.SemaphoreType.DMA((len(stages), 4)),
            pltpu.SemaphoreType.DMA((len(stages), 4)),
        ],
        compiler_params=pltpu.CompilerParams(collective_id=1, has_side_effects=True),
    )(value)


def on_device(hamiltonian, block_columns, potential, trial_slab):
    shard_blocks = hamiltonian.shape[0]
    block_size = hamiltonian.shape[2]
    states = trial_slab.shape[1]
    index = block_columns.reshape(-1)
    start_slab = trial_slab.reshape(shard_blocks, block_size, states)
    weights = potential.reshape(shard_blocks, block_size, 1)
    coupled_start = couple_all(hamiltonian, index, start_slab.astype(jnp.bfloat16))
    filtered_once = 0.5 * (coupled_start + weights * start_slab)
    coupled_next = couple_all(hamiltonian, index, filtered_once.astype(jnp.bfloat16))
    filtered = coupled_next + weights * filtered_once - start_slab
    flat = filtered.reshape(shard_blocks * block_size, states)
    rows_total = flat.shape[0] * lax.axis_size("group") * lax.axis_size("blk")
    local_gram = jnp.dot(flat.T, flat, precision=precise)
    gram = summed_over_mesh(local_gram) / rows_total
    lower = jnp.linalg.cholesky(gram)
    ortho_slab = lax.linalg.triangular_solve(
        lower, flat, left_side=False, lower=True, transpose_a=True
    )
    return (ortho_slab, jnp.transpose(lower))


def solution(mesh):
    placed = (
        P(("group", "blk"), None, None, None),
        P(("group", "blk"), None, None),
        P(("group", "blk")),
        P(("group", "blk"), None),
    )
    return jax.shard_map(
        on_device,
        mesh=mesh,
        in_specs=placed,
        out_specs=(P(("group", "blk"), None), P()),
        check_vma=False,
    )
```

```python
import functools

import jax
import jax.numpy as jnp
from jax import lax
from jax.experimental import pallas as pl
from jax.experimental.pallas import tpu as pltpu
from jax.sharding import PartitionSpec as P

precise = lax.Precision.HIGHEST
MESH = pl.DeviceIdType.MESH


RING = 4
QUARTERS = 4
NEIGHBOURS = (1, 3, 4, 12)


def forwards(t, q):
    tx, ty = t & 3, t >> 2
    out = []
    if q < 2:
        if t == 0:
            out += [1, 3]
        if ty == 0 and tx == 1 and q == 0:
            out.append(3)
        if ty == 0 and tx == 3 and q == 1:
            out.append(1)
        if ty == 0:
            out += [4, 12]
        if ty == 1 and q == 0:
            out.append(12)
        if ty == 3 and q == 1:
            out.append(4)
    else:
        if t == 0:
            out += [4, 12]
        if tx == 0 and ty == 1 and q == 2:
            out.append(12)
        if tx == 0 and ty == 3 and q == 3:
            out.append(4)
        if tx == 0:
            out += [1, 3]
        if tx == 1 and q == 2:
            out.append(3)
        if tx == 3 and q == 3:
            out.append(1)
    return out


def schedule():
    level = {(0, q): 0 for q in range(QUARTERS)}
    sends = []
    frontier = [(0, q) for q in range(QUARTERS)]
    while frontier:
        nxt = []
        for t, q in frontier:
            for d in forwards(t, q):
                dest = (t ^ d, q)
                assert dest not in level
                level[dest] = level[(t, q)] + 1
                sends.append((t, q, d))
                nxt.append(dest)
        frontier = nxt
    assert len(level) == RING * RING * QUARTERS
    return level, sends


def coupling_kernel(groups, index_ref, own_ref, ham_hbm, out_ref, *scratch):
    cycle = RING * RING
    held = scratch[: cycle + 1]
    ham_buf, ham_sem, send_sem, recv_sem, side_send, side_recv = scratch[cycle + 1 :]
    shard_blocks, nsrc, block_size, width = ham_hbm.shape
    per_source = width // block_size
    part = shard_blocks // QUARTERS
    me = lax.axis_index("blk")
    grp = lax.axis_index("group")
    has_below = grp > 0
    has_above = grp < groups - 1
    below_buf, above_buf = held[cycle - 1], held[cycle]
    level, sends = schedule()
    send_index = {item: k for k, item in enumerate(sends)}

    def buf(t):
        return own_ref if t == 0 else held[t - 1]

    def quarter(ref, q):
        return ref.at[pl.ds(q * part, part)]

    def link(t, q, d):
        return pltpu.make_async_remote_copy(
            src_ref=quarter(buf(t), q),
            dst_ref=quarter(buf(t ^ d), q),
            send_sem=send_sem.at[send_index[(t, q, d)]],
            recv_sem=recv_sem.at[t ^ d, q],
            device_id=(grp, me ^ d),
            device_id_type=MESH,
        )

    def arrival(t, q):
        return pltpu.make_async_remote_copy(
            src_ref=quarter(own_ref, q),
            dst_ref=quarter(buf(t), q),
            send_sem=side_send.at[0],
            recv_sem=recv_sem.at[t, q],
            device_id=(grp, me),
            device_id_type=MESH,
        )

    def side(k, device):
        dst = below_buf if k == 0 else above_buf
        return pltpu.make_async_remote_copy(
            src_ref=own_ref,
            dst_ref=dst,
            send_sem=side_send.at[k],
            recv_sem=side_recv.at[k],
            device_id=device,
            device_id_type=MESH,
        )

    barrier = pltpu.get_barrier_semaphore()
    for d in NEIGHBOURS:
        pl.semaphore_signal(barrier, inc=1, device_id=(grp, me ^ d), device_id_type=MESH)

    @pl.when(has_below)
    def _():
        pl.semaphore_signal(barrier, inc=1, device_id=(grp - 1, me), device_id_type=MESH)

    @pl.when(has_above)
    def _():
        pl.semaphore_signal(barrier, inc=1, device_id=(grp + 1, me), device_id_type=MESH)

    expected = len(NEIGHBOURS) + has_below.astype(jnp.int32) + has_above.astype(jnp.int32)
    pl.semaphore_wait(barrier, expected)

    for t, q, d in sends:
        if t == 0:
            link(t, q, d).start()

    @pl.when(has_above)
    def _():
        side(0, (grp + 1, me)).start()

    @pl.when(has_below)
    def _():
        side(1, (grp - 1, me)).start()

    top = max(level.values())
    steps = [("own", 0), ("below", nsrc - 2), ("above", nsrc - 1)]
    for lv in range(1, top + 1):
        ready = [t for t in range(1, cycle) if max(level[(t, q)] for q in range(QUARTERS)) == lv]
        steps.append(("arrive", lv))
        steps += [("slot", t) for t in ready]

    compute_steps = [s for s in steps if s[0] != "arrive"]

    def source_of(kind, t):
        if kind == "own":
            return me
        if kind == "slot":
            return me ^ t
        return t

    def ham_copy(i, slot):
        kind, t = compute_steps[i]
        return pltpu.make_async_copy(
            ham_hbm.at[:, source_of(kind, t)], ham_buf.at[slot], ham_sem.at[slot]
        )

    out_ref[...] = jnp.zeros_like(out_ref)
    ham_copy(0, 0).start()

    i = 0
    for kind, t in steps:
        if kind == "arrive":
            for (slot_t, q), v in sorted(level.items()):
                if v == t:
                    arrival(slot_t, q).wait_recv()
                    for d in forwards(slot_t, q):
                        link(slot_t, q, d).start()
            continue
        slot = i % 2
        if kind == "own":
            data = own_ref
        elif kind == "slot":
            data = buf(t)
        elif kind == "below":
            data = below_buf
        else:
            data = above_buf
        source = source_of(kind, t)

        def work(data=data, source=source, slot=slot, kind=kind):
            if kind == "below":
                side(0, (grp, me)).wait_recv()
            elif kind == "above":
                side(1, (grp, me)).wait_recv()

            def row(r, carry):
                blocks = [data[index_ref[(r * per_source + j) * nsrc + source]] for j in range(per_source)]
                picked = jnp.concatenate(blocks, axis=0)
                out_ref[r] += jnp.dot(
                    ham_buf[slot, r], picked, preferred_element_type=jnp.float32
                )
                return carry

            lax.fori_loop(0, shard_blocks, row, 0, unroll=True)

        ham_copy(i, slot).wait()
        if i + 1 < len(compute_steps):
            ham_copy(i + 1, 1 - slot).start()
        if kind == "below":
            pl.when(has_below)(work)
        elif kind == "above":
            pl.when(has_above)(work)
        else:
            work()
        i += 1

    for t, q, d in sends:
        link(t, q, d).wait_send()

    @pl.when(has_above)
    def _():
        side(0, (grp + 1, me)).wait_send()

    @pl.when(has_below)
    def _():
        side(1, (grp - 1, me)).wait_send()


def couple_all(hamiltonian, index, rounded):
    shard_blocks, nsrc, block_size, width = hamiltonian.shape
    states = rounded.shape[2]
    cycle = lax.axis_size("blk")
    assert cycle == RING * RING
    groups = lax.axis_size("group")
    slab = pltpu.VMEM(rounded.shape, rounded.dtype)
    flops = 2 * shard_blocks * nsrc * block_size * width * states
    return pl.pallas_call(
        functools.partial(coupling_kernel, groups),
        out_shape=jax.ShapeDtypeStruct((shard_blocks, block_size, states), jnp.float32),
        in_specs=[
            pl.BlockSpec(memory_space=pltpu.SMEM),
            pl.BlockSpec(memory_space=pltpu.VMEM),
            pl.BlockSpec(memory_space=pl.ANY),
        ],
        out_specs=pl.BlockSpec(memory_space=pltpu.VMEM),
        scratch_shapes=[slab] * (cycle + 1)
        + [
            pltpu.VMEM((2, shard_blocks, block_size, width), hamiltonian.dtype),
            pltpu.SemaphoreType.DMA((2,)),
            pltpu.SemaphoreType.DMA((len(schedule()[1]),)),
            pltpu.SemaphoreType.DMA((cycle, QUARTERS)),
            pltpu.SemaphoreType.DMA((2,)),
            pltpu.SemaphoreType.DMA((2,)),
        ],
        compiler_params=pltpu.CompilerParams(
            collective_id=0, has_side_effects=True, vmem_limit_bytes=48 * 1024 * 1024
        ),
        cost_estimate=pl.CostEstimate(
            flops=flops, transcendentals=0, bytes_accessed=hamiltonian.size * 2
        ),
    )(index, rounded, hamiltonian)


def gram_kernel(stages, gram_ref, out_ref, arrived, send_sem, recv_sem):
    place = {"group": lax.axis_index("group"), "blk": lax.axis_index("blk")}
    members = 4

    def field(axis, shift):
        return (place[axis] >> shift) % members

    def peer(axis, shift, position):
        other = dict(place)
        other[axis] = place[axis] + (position - field(axis, shift)) * (1 << shift)
        return (other["group"], other["blk"])

    barrier = pltpu.get_barrier_semaphore()
    for axis, shift in stages:
        for m in range(1, members):
            pl.semaphore_signal(
                barrier, inc=1, device_id=peer(axis, shift, field(axis, shift) ^ m), device_id_type=MESH
            )
    pl.semaphore_wait(barrier, len(stages) * (members - 1))
    out_ref[...] = gram_ref[...]
    for k, (axis, shift) in enumerate(stages):
        mine = field(axis, shift)

        def exchange(position, m):
            return pltpu.make_async_remote_copy(
                src_ref=out_ref,
                dst_ref=arrived.at[k, mine],
                send_sem=send_sem.at[k, m],
                recv_sem=recv_sem.at[k, mine],
                device_id=peer(axis, shift, position),
                device_id_type=MESH,
            )

        def incoming(position):
            return pltpu.make_async_remote_copy(
                src_ref=out_ref,
                dst_ref=arrived.at[k, position],
                send_sem=send_sem.at[k, 0],
                recv_sem=recv_sem.at[k, position],
                device_id=peer(axis, shift, position),
                device_id_type=MESH,
            )

        for m in range(1, members):
            exchange(mine ^ m, m).start()
        arrived[k, mine] = out_ref[...]
        for m in range(1, members):
            exchange(mine ^ m, m).wait_send()
        for m in range(1, members):
            incoming(mine ^ m).wait_recv()
        total = arrived[k, 0]
        for position in range(1, members):
            total = total + arrived[k, position]
        out_ref[...] = total


def summed_over_mesh(value):
    stages = []
    for axis in ("blk", "group"):
        size = lax.axis_size(axis)
        assert size == 16
        stages += [(axis, 0), (axis, 2)]
    return pl.pallas_call(
        functools.partial(gram_kernel, stages),
        out_shape=jax.ShapeDtypeStruct(value.shape, value.dtype),
        in_specs=[pl.BlockSpec(memory_space=pltpu.VMEM)],
        out_specs=pl.BlockSpec(memory_space=pltpu.VMEM),
        scratch_shapes=[
            pltpu.VMEM((len(stages), 4) + value.shape, value.dtype),
            pltpu.SemaphoreType.DMA((len(stages), 4)),
            pltpu.SemaphoreType.DMA((len(stages), 4)),
        ],
        compiler_params=pltpu.CompilerParams(collective_id=1, has_side_effects=True),
    )(value)


def on_device(hamiltonian, block_columns, potential, trial_slab):
    shard_blocks = hamiltonian.shape[0]
    block_size = hamiltonian.shape[2]
    states = trial_slab.shape[1]
    index = jnp.transpose(block_columns, (0, 2, 1)).reshape(-1)
    start_slab = trial_slab.reshape(shard_blocks, block_size, states)
    weights = potential.reshape(shard_blocks, block_size, 1)
    coupled_start = couple_all(hamiltonian, index, start_slab.astype(jnp.bfloat16))
    filtered_once = 0.5 * (coupled_start + weights * start_slab)
    coupled_next = couple_all(hamiltonian, index, filtered_once.astype(jnp.bfloat16))
    filtered = coupled_next + weights * filtered_once - start_slab
    flat = filtered.reshape(shard_blocks * block_size, states)
    rows_total = flat.shape[0] * lax.axis_size("group") * lax.axis_size("blk")
    local_gram = jnp.dot(flat.T, flat, precision=precise) * (1.0 / rows_total)
    gram = summed_over_mesh(local_gram)
    lower = lax.linalg.cholesky(gram, symmetrize_input=False)
    ortho_slab = lax.linalg.triangular_solve(
        lower, flat, left_side=False, lower=True, transpose_a=True
    )
    return (ortho_slab, jnp.transpose(lower))


def solution(mesh):
    placed = (
        P(("group", "blk"), None, None, None),
        P(("group", "blk"), None, None),
        P(("group", "blk")),
        P(("group", "blk"), None),
    )
    return jax.shard_map(
        on_device,
        mesh=mesh,
        in_specs=placed,
        out_specs=(P(("group", "blk"), None), P()),
        check_vma=False,
    )
```

```python
import functools

import jax
import jax.numpy as jnp
from jax import lax
from jax.experimental import pallas as pl
from jax.experimental.pallas import tpu as pltpu
from jax.sharding import PartitionSpec as P

precise = lax.Precision.HIGHEST
MESH = pl.DeviceIdType.MESH


RING = 4
QUARTERS = 4
NEIGHBOURS = (1, 3, 4, 12)


def forwards(t, q):
    tx, ty = t & 3, t >> 2
    out = []
    if q < 2:
        if t == 0:
            out += [1, 3]
        if ty == 0 and tx == 1 and q == 0:
            out.append(3)
        if ty == 0 and tx == 3 and q == 1:
            out.append(1)
        if ty == 0:
            out += [4, 12]
        if ty == 1 and q == 0:
            out.append(12)
        if ty == 3 and q == 1:
            out.append(4)
    else:
        if t == 0:
            out += [4, 12]
        if tx == 0 and ty == 1 and q == 2:
            out.append(12)
        if tx == 0 and ty == 3 and q == 3:
            out.append(4)
        if tx == 0:
            out += [1, 3]
        if tx == 1 and q == 2:
            out.append(3)
        if tx == 3 and q == 3:
            out.append(1)
    return out


def schedule():
    level = {(0, q): 0 for q in range(QUARTERS)}
    sends = []
    frontier = [(0, q) for q in range(QUARTERS)]
    while frontier:
        nxt = []
        for t, q in frontier:
            for d in forwards(t, q):
                dest = (t ^ d, q)
                assert dest not in level
                level[dest] = level[(t, q)] + 1
                sends.append((t, q, d))
                nxt.append(dest)
        frontier = nxt
    assert len(level) == RING * RING * QUARTERS
    return level, sends


def coupling_kernel(groups, index_ref, start_ref, scaled_ref, ham_hbm, once_ref, next_ref, *scratch):
    cycle = RING * RING
    held_sets = (scratch[: cycle + 1], scratch[cycle + 1 : 2 * cycle + 2])
    rounded, ham_buf, ham_sem, send_sem, recv_sem, side_send, side_recv = scratch[2 * cycle + 2 :]
    shard_blocks, nsrc, block_size, width = ham_hbm.shape
    per_source = width // block_size
    part = shard_blocks // QUARTERS
    me = lax.axis_index("blk")
    grp = lax.axis_index("group")
    has_below = grp > 0
    has_above = grp < groups - 1
    level, sends = schedule()
    send_index = {item: k for k, item in enumerate(sends)}
    owns = (start_ref, rounded)
    outs = (once_ref, next_ref)

    def buf(p, t):
        return owns[p] if t == 0 else held_sets[p][t - 1]

    def quarter(ref, q):
        return ref.at[pl.ds(q * part, part)]

    def link(p, t, q, d):
        return pltpu.make_async_remote_copy(
            src_ref=quarter(buf(p, t), q),
            dst_ref=quarter(buf(p, t ^ d), q),
            send_sem=send_sem.at[p, send_index[(t, q, d)]],
            recv_sem=recv_sem.at[p, t ^ d, q],
            device_id=(grp, me ^ d),
            device_id_type=MESH,
        )

    def arrival(p, t, q):
        return pltpu.make_async_remote_copy(
            src_ref=quarter(owns[p], q),
            dst_ref=quarter(buf(p, t), q),
            send_sem=side_send.at[p, 0],
            recv_sem=recv_sem.at[p, t, q],
            device_id=(grp, me),
            device_id_type=MESH,
        )

    def side(p, k, device):
        dst = held_sets[p][cycle - 1 + k]
        return pltpu.make_async_remote_copy(
            src_ref=owns[p],
            dst_ref=dst,
            send_sem=side_send.at[p, k],
            recv_sem=side_recv.at[p, k],
            device_id=device,
            device_id_type=MESH,
        )

    barrier = pltpu.get_barrier_semaphore()
    for d in NEIGHBOURS:
        pl.semaphore_signal(barrier, inc=1, device_id=(grp, me ^ d), device_id_type=MESH)

    @pl.when(has_below)
    def _():
        pl.semaphore_signal(barrier, inc=1, device_id=(grp - 1, me), device_id_type=MESH)

    @pl.when(has_above)
    def _():
        pl.semaphore_signal(barrier, inc=1, device_id=(grp + 1, me), device_id_type=MESH)

    expected = len(NEIGHBOURS) + has_below.astype(jnp.int32) + has_above.astype(jnp.int32)
    pl.semaphore_wait(barrier, expected)

    def send_own(p):
        for t, q, d in sends:
            if t == 0:
                link(p, t, q, d).start()

        @pl.when(has_above)
        def _():
            side(p, 0, (grp + 1, me)).start()

        @pl.when(has_below)
        def _():
            side(p, 1, (grp - 1, me)).start()

    top = max(level.values())
    steps = []
    for p in range(2):
        steps += [(p, "send", 0), (p, "own", 0), (p, "below", nsrc - 2), (p, "above", nsrc - 1)]
        for lv in range(1, top + 1):
            ready = [t for t in range(1, cycle) if max(level[(t, q)] for q in range(QUARTERS)) == lv]
            steps.append((p, "arrive", lv))
            steps += [(p, "slot", t) for t in ready]
        steps.append((p, "finish", 0))

    compute_steps = [x for x in steps if x[1] in ("own", "below", "above", "slot")]

    def source_of(kind, t):
        if kind == "own":
            return me
        if kind == "slot":
            return me ^ t
        return t

    def ham_copy(i, slot):
        p, kind, t = compute_steps[i]
        return pltpu.make_async_copy(
            ham_hbm.at[:, source_of(kind, t)], ham_buf.at[slot], ham_sem.at[slot]
        )

    once_ref[...] = jnp.zeros_like(once_ref)
    next_ref[...] = jnp.zeros_like(next_ref)
    ham_copy(0, 0).start()

    i = 0
    for p, kind, t in steps:
        if kind == "send":
            send_own(p)
            continue
        if kind == "arrive":
            for (slot_t, q), v in sorted(level.items()):
                if v == t:
                    arrival(p, slot_t, q).wait_recv()
                    for d in forwards(slot_t, q):
                        link(p, slot_t, q, d).start()
            continue
        if kind == "finish":
            if p == 0:
                once_ref[...] = 0.5 * (once_ref[...] + scaled_ref[...])
                rounded[...] = once_ref[...].astype(rounded.dtype)
            continue
        slot = i % 2
        if kind == "own":
            data = owns[p]
        elif kind == "slot":
            data = buf(p, t)
        elif kind == "below":
            data = held_sets[p][cycle - 1]
        else:
            data = held_sets[p][cycle]
        source = source_of(kind, t)
        out_ref = outs[p]

        def work(data=data, source=source, slot=slot, kind=kind, p=p, out_ref=out_ref):
            if kind == "below":
                side(p, 0, (grp, me)).wait_recv()
            elif kind == "above":
                side(p, 1, (grp, me)).wait_recv()

            def row(r, carry):
                blocks = [data[index_ref[(r * per_source + j) * nsrc + source]] for j in range(per_source)]
                picked = jnp.concatenate(blocks, axis=0)
                out_ref[r] += jnp.dot(
                    ham_buf[slot, r], picked, preferred_element_type=jnp.float32
                )
                return carry

            lax.fori_loop(0, shard_blocks, row, 0, unroll=True)

        ham_copy(i, slot).wait()
        if i + 1 < len(compute_steps):
            ham_copy(i + 1, 1 - slot).start()
        if kind == "below":
            pl.when(has_below)(work)
        elif kind == "above":
            pl.when(has_above)(work)
        else:
            work()
        i += 1

    for p in range(2):
        for t, q, d in sends:
            link(p, t, q, d).wait_send()

        @pl.when(has_above)
        def _():
            side(p, 0, (grp + 1, me)).wait_send()

        @pl.when(has_below)
        def _():
            side(p, 1, (grp - 1, me)).wait_send()


def couple_both(hamiltonian, index, start_round, scaled):
    shard_blocks, nsrc, block_size, width = hamiltonian.shape
    states = start_round.shape[2]
    cycle = lax.axis_size("blk")
    assert cycle == RING * RING
    groups = lax.axis_size("group")
    slab = pltpu.VMEM(start_round.shape, start_round.dtype)
    flops = 4 * shard_blocks * nsrc * block_size * width * states
    result = jax.ShapeDtypeStruct((shard_blocks, block_size, states), jnp.float32)
    vmem = pl.BlockSpec(memory_space=pltpu.VMEM)
    return pl.pallas_call(
        functools.partial(coupling_kernel, groups),
        out_shape=(result, result),
        in_specs=[pl.BlockSpec(memory_space=pltpu.SMEM), vmem, vmem, pl.BlockSpec(memory_space=pl.ANY)],
        out_specs=(vmem, vmem),
        scratch_shapes=[slab] * (2 * cycle + 2)
        + [
            slab,
            pltpu.VMEM((2, shard_blocks, block_size, width), hamiltonian.dtype),
            pltpu.SemaphoreType.DMA((2,)),
            pltpu.SemaphoreType.DMA((2, len(schedule()[1]))),
            pltpu.SemaphoreType.DMA((2, cycle, QUARTERS)),
            pltpu.SemaphoreType.DMA((2, 2)),
            pltpu.SemaphoreType.DMA((2, 2)),
        ],
        compiler_params=pltpu.CompilerParams(
            collective_id=0, has_side_effects=True, vmem_limit_bytes=48 * 1024 * 1024
        ),
        cost_estimate=pl.CostEstimate(
            flops=flops, transcendentals=0, bytes_accessed=hamiltonian.size * 4
        ),
    )(index, start_round, scaled, hamiltonian)


def gram_kernel(stages, gram_ref, out_ref, arrived, send_sem, recv_sem):
    place = {"group": lax.axis_index("group"), "blk": lax.axis_index("blk")}
    members = 4

    def field(axis, shift):
        return (place[axis] >> shift) % members

    def peer(axis, shift, position):
        other = dict(place)
        other[axis] = place[axis] + (position - field(axis, shift)) * (1 << shift)
        return (other["group"], other["blk"])

    barrier = pltpu.get_barrier_semaphore()
    for axis, shift in stages:
        for m in range(1, members):
            pl.semaphore_signal(
                barrier, inc=1, device_id=peer(axis, shift, field(axis, shift) ^ m), device_id_type=MESH
            )
    pl.semaphore_wait(barrier, len(stages) * (members - 1))
    out_ref[...] = gram_ref[...]
    for k, (axis, shift) in enumerate(stages):
        mine = field(axis, shift)

        def exchange(position, m):
            return pltpu.make_async_remote_copy(
                src_ref=out_ref,
                dst_ref=arrived.at[k, mine],
                send_sem=send_sem.at[k, m],
                recv_sem=recv_sem.at[k, mine],
                device_id=peer(axis, shift, position),
                device_id_type=MESH,
            )

        def incoming(position):
            return pltpu.make_async_remote_copy(
                src_ref=out_ref,
                dst_ref=arrived.at[k, position],
                send_sem=send_sem.at[k, 0],
                recv_sem=recv_sem.at[k, position],
                device_id=peer(axis, shift, position),
                device_id_type=MESH,
            )

        for m in range(1, members):
            exchange(mine ^ m, m).start()
        arrived[k, mine] = out_ref[...]
        for m in range(1, members):
            exchange(mine ^ m, m).wait_send()
        for m in range(1, members):
            incoming(mine ^ m).wait_recv()
        total = arrived[k, 0]
        for position in range(1, members):
            total = total + arrived[k, position]
        out_ref[...] = total


def summed_over_mesh(value):
    stages = []
    for axis in ("blk", "group"):
        size = lax.axis_size(axis)
        assert size == 16
        stages += [(axis, 0), (axis, 2)]
    return pl.pallas_call(
        functools.partial(gram_kernel, stages),
        out_shape=jax.ShapeDtypeStruct(value.shape, value.dtype),
        in_specs=[pl.BlockSpec(memory_space=pltpu.VMEM)],
        out_specs=pl.BlockSpec(memory_space=pltpu.VMEM),
        scratch_shapes=[
            pltpu.VMEM((len(stages), 4) + value.shape, value.dtype),
            pltpu.SemaphoreType.DMA((len(stages), 4)),
            pltpu.SemaphoreType.DMA((len(stages), 4)),
        ],
        compiler_params=pltpu.CompilerParams(collective_id=1, has_side_effects=True),
    )(value)


def on_device(hamiltonian, block_columns, potential, trial_slab):
    shard_blocks = hamiltonian.shape[0]
    block_size = hamiltonian.shape[2]
    states = trial_slab.shape[1]
    index = jnp.transpose(block_columns, (0, 2, 1)).reshape(-1)
    start_slab = trial_slab.reshape(shard_blocks, block_size, states)
    weights = potential.reshape(shard_blocks, block_size, 1)
    filtered_once, coupled_next = couple_both(
        hamiltonian, index, start_slab.astype(jnp.bfloat16), weights * start_slab
    )
    filtered = coupled_next + weights * filtered_once - start_slab
    flat = filtered.reshape(shard_blocks * block_size, states)
    rows_total = flat.shape[0] * lax.axis_size("group") * lax.axis_size("blk")
    local_gram = jnp.dot(flat.T, flat, precision=precise) * (1.0 / rows_total)
    gram = summed_over_mesh(local_gram)
    lower = lax.linalg.cholesky(gram, symmetrize_input=False)
    ortho_slab = lax.linalg.triangular_solve(
        lower, flat, left_side=False, lower=True, transpose_a=True
    )
    return (ortho_slab, jnp.transpose(lower))


def solution(mesh):
    placed = (
        P(("group", "blk"), None, None, None),
        P(("group", "blk"), None, None),
        P(("group", "blk")),
        P(("group", "blk"), None),
    )
    return jax.shard_map(
        on_device,
        mesh=mesh,
        in_specs=placed,
        out_specs=(P(("group", "blk"), None), P()),
        check_vma=False,
    )
```

```python
import functools

import jax
import jax.numpy as jnp
from jax import lax
from jax.experimental import pallas as pl
from jax.experimental.pallas import tpu as pltpu
from jax.sharding import PartitionSpec as P

precise = lax.Precision.HIGHEST
MESH = pl.DeviceIdType.MESH


RING = 4
QUARTERS = 4
NEIGHBOURS = (1, 3, 4, 12)


def forwards(t, q):
    tx, ty = t & 3, t >> 2
    out = []
    if q < 2:
        if t == 0:
            out += [1, 3]
        if ty == 0 and tx == 1 and q == 0:
            out.append(3)
        if ty == 0 and tx == 3 and q == 1:
            out.append(1)
        if ty == 0:
            out += [4, 12]
        if ty == 1 and q == 0:
            out.append(12)
        if ty == 3 and q == 1:
            out.append(4)
    else:
        if t == 0:
            out += [4, 12]
        if tx == 0 and ty == 1 and q == 2:
            out.append(12)
        if tx == 0 and ty == 3 and q == 3:
            out.append(4)
        if tx == 0:
            out += [1, 3]
        if tx == 1 and q == 2:
            out.append(3)
        if tx == 3 and q == 3:
            out.append(1)
    return out


def schedule():
    level = {(0, q): 0 for q in range(QUARTERS)}
    sends = []
    frontier = [(0, q) for q in range(QUARTERS)]
    while frontier:
        nxt = []
        for t, q in frontier:
            for d in forwards(t, q):
                dest = (t ^ d, q)
                assert dest not in level
                level[dest] = level[(t, q)] + 1
                sends.append((t, q, d))
                nxt.append(dest)
        frontier = nxt
    assert len(level) == RING * RING * QUARTERS
    return level, sends


def coupling_kernel(groups, index_ref, trial_ref, weight_ref, ham_hbm, once_ref, next_ref, *scratch):
    cycle = RING * RING
    held_sets = (scratch[: cycle + 1], scratch[cycle + 1 : 2 * cycle + 2])
    start_ref, rounded, ham_buf, ham_sem, send_sem, recv_sem, side_send, side_recv = scratch[2 * cycle + 2 :]
    shard_blocks, nsrc, block_size, width = ham_hbm.shape
    per_source = width // block_size
    part = shard_blocks // QUARTERS
    me = lax.axis_index("blk")
    grp = lax.axis_index("group")
    has_below = grp > 0
    has_above = grp < groups - 1
    level, sends = schedule()
    send_index = {item: k for k, item in enumerate(sends)}
    owns = (start_ref, rounded)
    outs = (once_ref, next_ref)

    def buf(p, t):
        return owns[p] if t == 0 else held_sets[p][t - 1]

    def quarter(ref, q):
        return ref.at[pl.ds(q * part, part)]

    def link(p, t, q, d):
        return pltpu.make_async_remote_copy(
            src_ref=quarter(buf(p, t), q),
            dst_ref=quarter(buf(p, t ^ d), q),
            send_sem=send_sem.at[p, send_index[(t, q, d)]],
            recv_sem=recv_sem.at[p, t ^ d, q],
            device_id=(grp, me ^ d),
            device_id_type=MESH,
        )

    def arrival(p, t, q):
        return pltpu.make_async_remote_copy(
            src_ref=quarter(owns[p], q),
            dst_ref=quarter(buf(p, t), q),
            send_sem=side_send.at[p, 0],
            recv_sem=recv_sem.at[p, t, q],
            device_id=(grp, me),
            device_id_type=MESH,
        )

    def side(p, k, device):
        dst = held_sets[p][cycle - 1 + k]
        return pltpu.make_async_remote_copy(
            src_ref=owns[p],
            dst_ref=dst,
            send_sem=side_send.at[p, k],
            recv_sem=side_recv.at[p, k],
            device_id=device,
            device_id_type=MESH,
        )

    start_ref[...] = trial_ref[...].astype(start_ref.dtype)
    barrier = pltpu.get_barrier_semaphore()
    for d in NEIGHBOURS:
        pl.semaphore_signal(barrier, inc=1, device_id=(grp, me ^ d), device_id_type=MESH)

    @pl.when(has_below)
    def _():
        pl.semaphore_signal(barrier, inc=1, device_id=(grp - 1, me), device_id_type=MESH)

    @pl.when(has_above)
    def _():
        pl.semaphore_signal(barrier, inc=1, device_id=(grp + 1, me), device_id_type=MESH)

    expected = len(NEIGHBOURS) + has_below.astype(jnp.int32) + has_above.astype(jnp.int32)
    pl.semaphore_wait(barrier, expected)

    def send_own(p):
        for t, q, d in sends:
            if t == 0:
                link(p, t, q, d).start()

        @pl.when(has_above)
        def _():
            side(p, 0, (grp + 1, me)).start()

        @pl.when(has_below)
        def _():
            side(p, 1, (grp - 1, me)).start()

    top = max(level.values())
    steps = []
    for p in range(2):
        steps += [(p, "send", 0), (p, "own", 0), (p, "below", nsrc - 2), (p, "above", nsrc - 1)]
        for lv in range(1, top + 1):
            ready = [t for t in range(1, cycle) if max(level[(t, q)] for q in range(QUARTERS)) == lv]
            steps.append((p, "arrive", lv))
            steps += [(p, "slot", t) for t in ready]
        steps.append((p, "finish", 0))

    compute_steps = [x for x in steps if x[1] in ("own", "below", "above", "slot")]

    def source_of(kind, t):
        if kind == "own":
            return me
        if kind == "slot":
            return me ^ t
        return t

    def ham_copy(i, slot):
        p, kind, t = compute_steps[i]
        return pltpu.make_async_copy(
            ham_hbm.at[:, source_of(kind, t)], ham_buf.at[slot], ham_sem.at[slot]
        )

    once_ref[...] = jnp.zeros_like(once_ref)
    next_ref[...] = jnp.zeros_like(next_ref)
    ham_copy(0, 0).start()

    i = 0
    for p, kind, t in steps:
        if kind == "send":
            send_own(p)
            continue
        if kind == "arrive":
            for (slot_t, q), v in sorted(level.items()):
                if v == t:
                    arrival(p, slot_t, q).wait_recv()
                    for d in forwards(slot_t, q):
                        link(p, slot_t, q, d).start()
            continue
        if kind == "finish":
            if p == 0:
                once_ref[...] = 0.5 * (once_ref[...] + weight_ref[...] * trial_ref[...])
                rounded[...] = once_ref[...].astype(rounded.dtype)
            continue
        slot = i % 2
        if kind == "own":
            data = owns[p]
        elif kind == "slot":
            data = buf(p, t)
        elif kind == "below":
            data = held_sets[p][cycle - 1]
        else:
            data = held_sets[p][cycle]
        source = source_of(kind, t)
        out_ref = outs[p]

        def work(data=data, source=source, slot=slot, kind=kind, p=p, out_ref=out_ref):
            if kind == "below":
                side(p, 0, (grp, me)).wait_recv()
            elif kind == "above":
                side(p, 1, (grp, me)).wait_recv()

            def row(r, carry):
                blocks = [data[index_ref[(r * per_source + j) * nsrc + source]] for j in range(per_source)]
                picked = jnp.concatenate(blocks, axis=0)
                out_ref[r] += jnp.dot(
                    ham_buf[slot, r], picked, preferred_element_type=jnp.float32
                )
                return carry

            lax.fori_loop(0, shard_blocks, row, 0, unroll=True)

        ham_copy(i, slot).wait()
        if i + 1 < len(compute_steps):
            ham_copy(i + 1, 1 - slot).start()
        if kind == "below":
            pl.when(has_below)(work)
        elif kind == "above":
            pl.when(has_above)(work)
        else:
            work()
        i += 1

    for p in range(2):
        for t, q, d in sends:
            link(p, t, q, d).wait_send()

        @pl.when(has_above)
        def _():
            side(p, 0, (grp + 1, me)).wait_send()

        @pl.when(has_below)
        def _():
            side(p, 1, (grp - 1, me)).wait_send()


def couple_both(hamiltonian, index, trial, weights):
    shard_blocks, nsrc, block_size, width = hamiltonian.shape
    states = trial.shape[2]
    cycle = lax.axis_size("blk")
    assert cycle == RING * RING
    groups = lax.axis_size("group")
    slab = pltpu.VMEM(trial.shape, jnp.bfloat16)
    flops = 4 * shard_blocks * nsrc * block_size * width * states
    result = jax.ShapeDtypeStruct((shard_blocks, block_size, states), jnp.float32)
    vmem = pl.BlockSpec(memory_space=pltpu.VMEM)
    return pl.pallas_call(
        functools.partial(coupling_kernel, groups),
        out_shape=(result, result),
        in_specs=[pl.BlockSpec(memory_space=pltpu.SMEM), vmem, vmem, pl.BlockSpec(memory_space=pl.ANY)],
        out_specs=(vmem, vmem),
        scratch_shapes=[slab] * (2 * cycle + 2)
        + [
            slab,
            slab,
            pltpu.VMEM((2, shard_blocks, block_size, width), hamiltonian.dtype),
            pltpu.SemaphoreType.DMA((2,)),
            pltpu.SemaphoreType.DMA((2, len(schedule()[1]))),
            pltpu.SemaphoreType.DMA((2, cycle, QUARTERS)),
            pltpu.SemaphoreType.DMA((2, 2)),
            pltpu.SemaphoreType.DMA((2, 2)),
        ],
        compiler_params=pltpu.CompilerParams(
            collective_id=0, has_side_effects=True, vmem_limit_bytes=48 * 1024 * 1024
        ),
        cost_estimate=pl.CostEstimate(
            flops=flops, transcendentals=0, bytes_accessed=hamiltonian.size * 4
        ),
    )(index, trial, weights, hamiltonian)


def gram_kernel(stages, gram_ref, out_ref, arrived, send_sem, recv_sem):
    place = {"group": lax.axis_index("group"), "blk": lax.axis_index("blk")}
    members = 4

    def field(axis, shift):
        return (place[axis] >> shift) % members

    def peer(axis, shift, position):
        other = dict(place)
        other[axis] = place[axis] + (position - field(axis, shift)) * (1 << shift)
        return (other["group"], other["blk"])

    barrier = pltpu.get_barrier_semaphore()
    for axis, shift in stages:
        for m in range(1, members):
            pl.semaphore_signal(
                barrier, inc=1, device_id=peer(axis, shift, field(axis, shift) ^ m), device_id_type=MESH
            )
    pl.semaphore_wait(barrier, len(stages) * (members - 1))
    out_ref[...] = gram_ref[...]
    for k, (axis, shift) in enumerate(stages):
        mine = field(axis, shift)

        def exchange(position, m):
            return pltpu.make_async_remote_copy(
                src_ref=out_ref,
                dst_ref=arrived.at[k, mine],
                send_sem=send_sem.at[k, m],
                recv_sem=recv_sem.at[k, mine],
                device_id=peer(axis, shift, position),
                device_id_type=MESH,
            )

        def incoming(position):
            return pltpu.make_async_remote_copy(
                src_ref=out_ref,
                dst_ref=arrived.at[k, position],
                send_sem=send_sem.at[k, 0],
                recv_sem=recv_sem.at[k, position],
                device_id=peer(axis, shift, position),
                device_id_type=MESH,
            )

        for m in range(1, members):
            exchange(mine ^ m, m).start()
        arrived[k, mine] = out_ref[...]
        for m in range(1, members):
            exchange(mine ^ m, m).wait_send()
        for m in range(1, members):
            incoming(mine ^ m).wait_recv()
        total = arrived[k, 0]
        for position in range(1, members):
            total = total + arrived[k, position]
        out_ref[...] = total


def summed_over_mesh(value):
    stages = []
    for axis in ("blk", "group"):
        size = lax.axis_size(axis)
        assert size == 16
        stages += [(axis, 0), (axis, 2)]
    return pl.pallas_call(
        functools.partial(gram_kernel, stages),
        out_shape=jax.ShapeDtypeStruct(value.shape, value.dtype),
        in_specs=[pl.BlockSpec(memory_space=pltpu.VMEM)],
        out_specs=pl.BlockSpec(memory_space=pltpu.VMEM),
        scratch_shapes=[
            pltpu.VMEM((len(stages), 4) + value.shape, value.dtype),
            pltpu.SemaphoreType.DMA((len(stages), 4)),
            pltpu.SemaphoreType.DMA((len(stages), 4)),
        ],
        compiler_params=pltpu.CompilerParams(collective_id=1, has_side_effects=True),
    )(value)


def on_device(hamiltonian, block_columns, potential, trial_slab):
    shard_blocks = hamiltonian.shape[0]
    block_size = hamiltonian.shape[2]
    states = trial_slab.shape[1]
    index = jnp.transpose(block_columns, (0, 2, 1)).reshape(-1)
    start_slab = trial_slab.reshape(shard_blocks, block_size, states)
    weights = potential.reshape(shard_blocks, block_size, 1)
    filtered_once, coupled_next = couple_both(hamiltonian, index, start_slab, weights)
    filtered = coupled_next + weights * filtered_once - start_slab
    flat = filtered.reshape(shard_blocks * block_size, states)
    rows_total = flat.shape[0] * lax.axis_size("group") * lax.axis_size("blk")
    local_gram = jnp.dot(flat.T, flat, precision=precise) * (1.0 / rows_total)
    gram = summed_over_mesh(local_gram)
    lower = lax.linalg.cholesky(gram, symmetrize_input=False)
    ortho_slab = lax.linalg.triangular_solve(
        lower, flat, left_side=False, lower=True, transpose_a=True
    )
    return (ortho_slab, jnp.transpose(lower))


def solution(mesh):
    placed = (
        P(("group", "blk"), None, None, None),
        P(("group", "blk"), None, None),
        P(("group", "blk")),
        P(("group", "blk"), None),
    )
    return jax.shard_map(
        on_device,
        mesh=mesh,
        in_specs=placed,
        out_specs=(P(("group", "blk"), None), P()),
        check_vma=False,
    )
```

```python
import functools

import jax
import jax.numpy as jnp
from jax import lax
from jax.experimental import pallas as pl
from jax.experimental.pallas import tpu as pltpu
from jax.sharding import PartitionSpec as P

precise = lax.Precision.HIGHEST
MESH = pl.DeviceIdType.MESH


RING = 4
QUARTERS = 4
NEIGHBOURS = (1, 3, 4, 12)


def forwards(t, q):
    tx, ty = t & 3, t >> 2
    out = []
    if q < 2:
        if t == 0:
            out += [1, 3]
        if ty == 0 and tx == 1 and q == 0:
            out.append(3)
        if ty == 0 and tx == 3 and q == 1:
            out.append(1)
        if ty == 0:
            out += [4, 12]
        if ty == 1 and q == 0:
            out.append(12)
        if ty == 3 and q == 1:
            out.append(4)
    else:
        if t == 0:
            out += [4, 12]
        if tx == 0 and ty == 1 and q == 2:
            out.append(12)
        if tx == 0 and ty == 3 and q == 3:
            out.append(4)
        if tx == 0:
            out += [1, 3]
        if tx == 1 and q == 2:
            out.append(3)
        if tx == 3 and q == 3:
            out.append(1)
    return out


def schedule():
    level = {(0, q): 0 for q in range(QUARTERS)}
    sends = []
    frontier = [(0, q) for q in range(QUARTERS)]
    while frontier:
        nxt = []
        for t, q in frontier:
            for d in forwards(t, q):
                dest = (t ^ d, q)
                assert dest not in level
                level[dest] = level[(t, q)] + 1
                sends.append((t, q, d))
                nxt.append(dest)
        frontier = nxt
    assert len(level) == RING * RING * QUARTERS
    return level, sends


def coupling_kernel(groups, index_ref, trial_ref, weight_ref, ham_hbm, once_ref, next_ref, *scratch):
    cycle = RING * RING
    held_sets = (scratch[: cycle + 1], scratch[cycle + 1 : 2 * cycle + 2])
    start_ref, rounded, ham_buf, ham_sem, send_sem, recv_sem, side_send, side_recv = scratch[2 * cycle + 2 :]
    shard_blocks, nsrc, block_size, width = ham_hbm.shape
    per_source = width // block_size
    part = shard_blocks // QUARTERS
    me = lax.axis_index("blk")
    grp = lax.axis_index("group")
    has_below = grp > 0
    has_above = grp < groups - 1
    level, sends = schedule()
    send_index = {item: k for k, item in enumerate(sends)}
    owns = (start_ref, rounded)
    outs = (once_ref, next_ref)

    def buf(p, t):
        return owns[p] if t == 0 else held_sets[p][t - 1]

    def quarter(ref, q):
        return ref.at[pl.ds(q * part, part)]

    def link(p, t, q, d):
        return pltpu.make_async_remote_copy(
            src_ref=quarter(buf(p, t), q),
            dst_ref=quarter(buf(p, t ^ d), q),
            send_sem=send_sem.at[p, send_index[(t, q, d)]],
            recv_sem=recv_sem.at[p, t ^ d, q],
            device_id=(grp, me ^ d),
            device_id_type=MESH,
        )

    def arrival(p, t, q):
        return pltpu.make_async_remote_copy(
            src_ref=quarter(owns[p], q),
            dst_ref=quarter(buf(p, t), q),
            send_sem=side_send.at[p, 0],
            recv_sem=recv_sem.at[p, t, q],
            device_id=(grp, me),
            device_id_type=MESH,
        )

    def side(p, k, device):
        dst = held_sets[p][cycle - 1 + k]
        return pltpu.make_async_remote_copy(
            src_ref=owns[p],
            dst_ref=dst,
            send_sem=side_send.at[p, k],
            recv_sem=side_recv.at[p, k],
            device_id=device,
            device_id_type=MESH,
        )

    start_ref[...] = trial_ref[...].astype(start_ref.dtype)
    barrier = pltpu.get_barrier_semaphore()
    for d in NEIGHBOURS:
        pl.semaphore_signal(barrier, inc=1, device_id=(grp, me ^ d), device_id_type=MESH)

    @pl.when(has_below)
    def _():
        pl.semaphore_signal(barrier, inc=1, device_id=(grp - 1, me), device_id_type=MESH)

    @pl.when(has_above)
    def _():
        pl.semaphore_signal(barrier, inc=1, device_id=(grp + 1, me), device_id_type=MESH)

    expected = len(NEIGHBOURS) + has_below.astype(jnp.int32) + has_above.astype(jnp.int32)
    pl.semaphore_wait(barrier, expected)

    def send_own(p):
        for t, q, d in sends:
            if t == 0:
                link(p, t, q, d).start()

        @pl.when(has_above)
        def _():
            side(p, 0, (grp + 1, me)).start()

        @pl.when(has_below)
        def _():
            side(p, 1, (grp - 1, me)).start()

    top = max(level.values())
    steps = []
    for p in range(2):
        steps += [(p, "send", 0), (p, "own", 0), (p, "below", nsrc - 2), (p, "above", nsrc - 1)]
        for lv in range(1, top + 1):
            ready = [t for t in range(1, cycle) if max(level[(t, q)] for q in range(QUARTERS)) == lv]
            steps.append((p, "arrive", lv))
            steps += [(p, "slot", t) for t in ready]
        steps.append((p, "finish", 0))

    compute_steps = [x for x in steps if x[1] in ("own", "below", "above", "slot")]

    def source_of(kind, t):
        if kind == "own":
            return me
        if kind == "slot":
            return me ^ t
        return t

    def ham_copy(i, slot):
        p, kind, t = compute_steps[i]
        return pltpu.make_async_copy(
            ham_hbm.at[:, source_of(kind, t)], ham_buf.at[slot], ham_sem.at[slot]
        )

    once_ref[...] = jnp.zeros_like(once_ref)
    next_ref[...] = jnp.zeros_like(next_ref)
    ham_copy(0, 0).start()

    i = 0
    for p, kind, t in steps:
        if kind == "send":
            send_own(p)
            continue
        if kind == "arrive":
            for (slot_t, q), v in sorted(level.items()):
                if v == t:
                    arrival(p, slot_t, q).wait_recv()
                    for d in forwards(slot_t, q):
                        link(p, slot_t, q, d).start()
            continue
        if kind == "finish":
            if p == 0:
                once_ref[...] = 0.5 * (once_ref[...] + weight_ref[...] * trial_ref[...])
                rounded[...] = once_ref[...].astype(rounded.dtype)
            else:
                next_ref[...] = next_ref[...] + weight_ref[...] * once_ref[...] - trial_ref[...]
            continue
        slot = i % 2
        if kind == "own":
            data = owns[p]
        elif kind == "slot":
            data = buf(p, t)
        elif kind == "below":
            data = held_sets[p][cycle - 1]
        else:
            data = held_sets[p][cycle]
        source = source_of(kind, t)
        out_ref = outs[p]

        def work(data=data, source=source, slot=slot, kind=kind, p=p, out_ref=out_ref):
            if kind == "below":
                side(p, 0, (grp, me)).wait_recv()
            elif kind == "above":
                side(p, 1, (grp, me)).wait_recv()

            def row(r, carry):
                blocks = [data[index_ref[(r * per_source + j) * nsrc + source]] for j in range(per_source)]
                picked = jnp.concatenate(blocks, axis=0)
                out_ref[r] += jnp.dot(
                    ham_buf[slot, r], picked, preferred_element_type=jnp.float32
                )
                return carry

            lax.fori_loop(0, shard_blocks, row, 0, unroll=True)

        ham_copy(i, slot).wait()
        if i + 1 < len(compute_steps):
            ham_copy(i + 1, 1 - slot).start()
        if kind == "below":
            pl.when(has_below)(work)
        elif kind == "above":
            pl.when(has_above)(work)
        else:
            work()
        i += 1

    for p in range(2):
        for t, q, d in sends:
            link(p, t, q, d).wait_send()

        @pl.when(has_above)
        def _():
            side(p, 0, (grp + 1, me)).wait_send()

        @pl.when(has_below)
        def _():
            side(p, 1, (grp - 1, me)).wait_send()


def couple_both(hamiltonian, index, trial, weights):
    shard_blocks, nsrc, block_size, width = hamiltonian.shape
    states = trial.shape[2]
    cycle = lax.axis_size("blk")
    assert cycle == RING * RING
    groups = lax.axis_size("group")
    slab = pltpu.VMEM(trial.shape, jnp.bfloat16)
    flops = 4 * shard_blocks * nsrc * block_size * width * states
    result = jax.ShapeDtypeStruct((shard_blocks, block_size, states), jnp.float32)
    vmem = pl.BlockSpec(memory_space=pltpu.VMEM)
    return pl.pallas_call(
        functools.partial(coupling_kernel, groups),
        out_shape=(result, result),
        in_specs=[pl.BlockSpec(memory_space=pltpu.SMEM), vmem, vmem, pl.BlockSpec(memory_space=pl.ANY)],
        out_specs=(vmem, vmem),
        scratch_shapes=[slab] * (2 * cycle + 2)
        + [
            slab,
            slab,
            pltpu.VMEM((2, shard_blocks, block_size, width), hamiltonian.dtype),
            pltpu.SemaphoreType.DMA((2,)),
            pltpu.SemaphoreType.DMA((2, len(schedule()[1]))),
            pltpu.SemaphoreType.DMA((2, cycle, QUARTERS)),
            pltpu.SemaphoreType.DMA((2, 2)),
            pltpu.SemaphoreType.DMA((2, 2)),
        ],
        compiler_params=pltpu.CompilerParams(
            collective_id=0, has_side_effects=True, vmem_limit_bytes=48 * 1024 * 1024
        ),
        cost_estimate=pl.CostEstimate(
            flops=flops, transcendentals=0, bytes_accessed=hamiltonian.size * 4
        ),
    )(index, trial, weights, hamiltonian)


def gram_kernel(stages, gram_ref, out_ref, arrived, send_sem, recv_sem):
    place = {"group": lax.axis_index("group"), "blk": lax.axis_index("blk")}
    members = 4

    def field(axis, shift):
        return (place[axis] >> shift) % members

    def peer(axis, shift, position):
        other = dict(place)
        other[axis] = place[axis] + (position - field(axis, shift)) * (1 << shift)
        return (other["group"], other["blk"])

    barrier = pltpu.get_barrier_semaphore()
    for axis, shift in stages:
        for m in range(1, members):
            pl.semaphore_signal(
                barrier, inc=1, device_id=peer(axis, shift, field(axis, shift) ^ m), device_id_type=MESH
            )
    pl.semaphore_wait(barrier, len(stages) * (members - 1))
    out_ref[...] = gram_ref[...]
    for k, (axis, shift) in enumerate(stages):
        mine = field(axis, shift)

        def exchange(position, m):
            return pltpu.make_async_remote_copy(
                src_ref=out_ref,
                dst_ref=arrived.at[k, mine],
                send_sem=send_sem.at[k, m],
                recv_sem=recv_sem.at[k, mine],
                device_id=peer(axis, shift, position),
                device_id_type=MESH,
            )

        def incoming(position):
            return pltpu.make_async_remote_copy(
                src_ref=out_ref,
                dst_ref=arrived.at[k, position],
                send_sem=send_sem.at[k, 0],
                recv_sem=recv_sem.at[k, position],
                device_id=peer(axis, shift, position),
                device_id_type=MESH,
            )

        for m in range(1, members):
            exchange(mine ^ m, m).start()
        arrived[k, mine] = out_ref[...]
        for m in range(1, members):
            exchange(mine ^ m, m).wait_send()
        for m in range(1, members):
            incoming(mine ^ m).wait_recv()
        total = arrived[k, 0]
        for position in range(1, members):
            total = total + arrived[k, position]
        out_ref[...] = total


def summed_over_mesh(value):
    stages = []
    for axis in ("blk", "group"):
        size = lax.axis_size(axis)
        assert size == 16
        stages += [(axis, 0), (axis, 2)]
    return pl.pallas_call(
        functools.partial(gram_kernel, stages),
        out_shape=jax.ShapeDtypeStruct(value.shape, value.dtype),
        in_specs=[pl.BlockSpec(memory_space=pltpu.VMEM)],
        out_specs=pl.BlockSpec(memory_space=pltpu.VMEM),
        scratch_shapes=[
            pltpu.VMEM((len(stages), 4) + value.shape, value.dtype),
            pltpu.SemaphoreType.DMA((len(stages), 4)),
            pltpu.SemaphoreType.DMA((len(stages), 4)),
        ],
        compiler_params=pltpu.CompilerParams(collective_id=1, has_side_effects=True),
    )(value)


def on_device(hamiltonian, block_columns, potential, trial_slab):
    shard_blocks = hamiltonian.shape[0]
    block_size = hamiltonian.shape[2]
    states = trial_slab.shape[1]
    index = jnp.transpose(block_columns, (0, 2, 1)).reshape(-1)
    start_slab = trial_slab.reshape(shard_blocks, block_size, states)
    weights = potential.reshape(shard_blocks, block_size, 1)
    filtered_once, filtered = couple_both(hamiltonian, index, start_slab, weights)
    flat = filtered.reshape(shard_blocks * block_size, states)
    rows_total = flat.shape[0] * lax.axis_size("group") * lax.axis_size("blk")
    local_gram = jnp.dot(flat.T, flat, precision=precise) * (1.0 / rows_total)
    gram = summed_over_mesh(local_gram)
    lower = lax.linalg.cholesky(gram, symmetrize_input=False)
    ortho_slab = lax.linalg.triangular_solve(
        lower, flat, left_side=False, lower=True, transpose_a=True
    )
    return (ortho_slab, jnp.transpose(lower))


def solution(mesh):
    placed = (
        P(("group", "blk"), None, None, None),
        P(("group", "blk"), None, None),
        P(("group", "blk")),
        P(("group", "blk"), None),
    )
    return jax.shard_map(
        on_device,
        mesh=mesh,
        in_specs=placed,
        out_specs=(P(("group", "blk"), None), P()),
        check_vma=False,
    )
```

```python
import functools

import jax
import jax.numpy as jnp
from jax import lax
from jax.experimental import pallas as pl
from jax.experimental.pallas import tpu as pltpu
from jax.sharding import PartitionSpec as P

precise = lax.Precision.HIGHEST
MESH = pl.DeviceIdType.MESH


RING = 4
QUARTERS = 4
NEIGHBOURS = (1, 3, 4, 12)


def forwards(t, q):
    tx, ty = t & 3, t >> 2
    out = []
    if q < 2:
        if t == 0:
            out += [1, 3]
        if ty == 0 and tx == 1 and q == 0:
            out.append(3)
        if ty == 0 and tx == 3 and q == 1:
            out.append(1)
        if ty == 0:
            out += [4, 12]
        if ty == 1 and q == 0:
            out.append(12)
        if ty == 3 and q == 1:
            out.append(4)
    else:
        if t == 0:
            out += [4, 12]
        if tx == 0 and ty == 1 and q == 2:
            out.append(12)
        if tx == 0 and ty == 3 and q == 3:
            out.append(4)
        if tx == 0:
            out += [1, 3]
        if tx == 1 and q == 2:
            out.append(3)
        if tx == 3 and q == 3:
            out.append(1)
    return out


def schedule():
    level = {(0, q): 0 for q in range(QUARTERS)}
    sends = []
    frontier = [(0, q) for q in range(QUARTERS)]
    while frontier:
        nxt = []
        for t, q in frontier:
            for d in forwards(t, q):
                dest = (t ^ d, q)
                assert dest not in level
                level[dest] = level[(t, q)] + 1
                sends.append((t, q, d))
                nxt.append(dest)
        frontier = nxt
    assert len(level) == RING * RING * QUARTERS
    return level, sends


def coupling_kernel(groups, scale, index_ref, trial_ref, weight_ref, ham_hbm, once_ref, next_ref, gram_ref, *scratch):
    cycle = RING * RING
    held_sets = (scratch[: cycle + 1], scratch[cycle + 1 : 2 * cycle + 2])
    start_ref, rounded, ham_buf, ham_sem, send_sem, recv_sem, side_send, side_recv, arrived, g_send, g_recv = scratch[2 * cycle + 2 :]
    shard_blocks, nsrc, block_size, width = ham_hbm.shape
    per_source = width // block_size
    part = shard_blocks // QUARTERS
    me = lax.axis_index("blk")
    grp = lax.axis_index("group")
    has_below = grp > 0
    has_above = grp < groups - 1
    level, sends = schedule()
    send_index = {item: k for k, item in enumerate(sends)}
    owns = (start_ref, rounded)
    outs = (once_ref, next_ref)

    def buf(p, t):
        return owns[p] if t == 0 else held_sets[p][t - 1]

    def quarter(ref, q):
        return ref.at[pl.ds(q * part, part)]

    def link(p, t, q, d):
        return pltpu.make_async_remote_copy(
            src_ref=quarter(buf(p, t), q),
            dst_ref=quarter(buf(p, t ^ d), q),
            send_sem=send_sem.at[p, send_index[(t, q, d)]],
            recv_sem=recv_sem.at[p, t ^ d, q],
            device_id=(grp, me ^ d),
            device_id_type=MESH,
        )

    def arrival(p, t, q):
        return pltpu.make_async_remote_copy(
            src_ref=quarter(owns[p], q),
            dst_ref=quarter(buf(p, t), q),
            send_sem=side_send.at[p, 0],
            recv_sem=recv_sem.at[p, t, q],
            device_id=(grp, me),
            device_id_type=MESH,
        )

    def side(p, k, device):
        dst = held_sets[p][cycle - 1 + k]
        return pltpu.make_async_remote_copy(
            src_ref=owns[p],
            dst_ref=dst,
            send_sem=side_send.at[p, k],
            recv_sem=side_recv.at[p, k],
            device_id=device,
            device_id_type=MESH,
        )

    start_ref[...] = trial_ref[...].astype(start_ref.dtype)
    barrier = pltpu.get_barrier_semaphore()
    for d in NEIGHBOURS:
        pl.semaphore_signal(barrier, inc=1, device_id=(grp, me ^ d), device_id_type=MESH)

    @pl.when(has_below)
    def _():
        pl.semaphore_signal(barrier, inc=1, device_id=(grp - 1, me), device_id_type=MESH)

    @pl.when(has_above)
    def _():
        pl.semaphore_signal(barrier, inc=1, device_id=(grp + 1, me), device_id_type=MESH)

    place = {"group": grp, "blk": me}
    stages = [("blk", 0), ("blk", 2), ("group", 0), ("group", 2)]

    def field(axis, shift):
        return (place[axis] >> shift) % QUARTERS

    def peer(axis, shift, position):
        other = dict(place)
        other[axis] = place[axis] + (position - field(axis, shift)) * (1 << shift)
        return (other["group"], other["blk"])

    for axis, shift in stages:
        for m in range(1, QUARTERS):
            pl.semaphore_signal(
                barrier, inc=1, device_id=peer(axis, shift, field(axis, shift) ^ m), device_id_type=MESH
            )
    expected = len(NEIGHBOURS) + has_below.astype(jnp.int32) + has_above.astype(jnp.int32)
    pl.semaphore_wait(barrier, expected + len(stages) * (QUARTERS - 1))

    def send_own(p):
        for t, q, d in sends:
            if t == 0:
                link(p, t, q, d).start()

        @pl.when(has_above)
        def _():
            side(p, 0, (grp + 1, me)).start()

        @pl.when(has_below)
        def _():
            side(p, 1, (grp - 1, me)).start()

    top = max(level.values())
    steps = []
    for p in range(2):
        steps += [(p, "send", 0), (p, "own", 0), (p, "below", nsrc - 2), (p, "above", nsrc - 1)]
        for lv in range(1, top + 1):
            ready = [t for t in range(1, cycle) if max(level[(t, q)] for q in range(QUARTERS)) == lv]
            steps.append((p, "arrive", lv))
            steps += [(p, "slot", t) for t in ready]
        steps.append((p, "finish", 0))

    compute_steps = [x for x in steps if x[1] in ("own", "below", "above", "slot")]

    def source_of(kind, t):
        if kind == "own":
            return me
        if kind == "slot":
            return me ^ t
        return t

    def ham_copy(i, slot):
        p, kind, t = compute_steps[i]
        return pltpu.make_async_copy(
            ham_hbm.at[:, source_of(kind, t)], ham_buf.at[slot], ham_sem.at[slot]
        )

    once_ref[...] = jnp.zeros_like(once_ref)
    next_ref[...] = jnp.zeros_like(next_ref)
    ham_copy(0, 0).start()

    i = 0
    for p, kind, t in steps:
        if kind == "send":
            send_own(p)
            continue
        if kind == "arrive":
            for (slot_t, q), v in sorted(level.items()):
                if v == t:
                    arrival(p, slot_t, q).wait_recv()
                    for d in forwards(slot_t, q):
                        link(p, slot_t, q, d).start()
            continue
        if kind == "finish":
            if p == 0:
                once_ref[...] = 0.5 * (once_ref[...] + weight_ref[...] * trial_ref[...])
                rounded[...] = once_ref[...].astype(rounded.dtype)
            else:
                next_ref[...] = next_ref[...] + weight_ref[...] * once_ref[...] - trial_ref[...]
                local = jnp.zeros(gram_ref.shape, jnp.float32)
                for r in range(shard_blocks):
                    rows = next_ref[r]
                    local = local + jnp.dot(
                        rows.T, rows, precision=lax.Precision.HIGHEST, preferred_element_type=jnp.float32
                    )
                gram_ref[...] = local * scale
            continue
        slot = i % 2
        if kind == "own":
            data = owns[p]
        elif kind == "slot":
            data = buf(p, t)
        elif kind == "below":
            data = held_sets[p][cycle - 1]
        else:
            data = held_sets[p][cycle]
        source = source_of(kind, t)
        out_ref = outs[p]

        def work(data=data, source=source, slot=slot, kind=kind, p=p, out_ref=out_ref):
            if kind == "below":
                side(p, 0, (grp, me)).wait_recv()
            elif kind == "above":
                side(p, 1, (grp, me)).wait_recv()

            def row(r, carry):
                blocks = [data[index_ref[(r * per_source + j) * nsrc + source]] for j in range(per_source)]
                picked = jnp.concatenate(blocks, axis=0)
                out_ref[r] += jnp.dot(
                    ham_buf[slot, r], picked, preferred_element_type=jnp.float32
                )
                return carry

            lax.fori_loop(0, shard_blocks, row, 0, unroll=True)

        ham_copy(i, slot).wait()
        if i + 1 < len(compute_steps):
            ham_copy(i + 1, 1 - slot).start()
        if kind == "below":
            pl.when(has_below)(work)
        elif kind == "above":
            pl.when(has_above)(work)
        else:
            work()
        i += 1

    for k, (axis, shift) in enumerate(stages):
        mine = field(axis, shift)

        def exchange(position, m):
            return pltpu.make_async_remote_copy(
                src_ref=gram_ref,
                dst_ref=arrived.at[k, mine],
                send_sem=g_send.at[k, m],
                recv_sem=g_recv.at[k, mine],
                device_id=peer(axis, shift, position),
                device_id_type=MESH,
            )

        def incoming(position):
            return pltpu.make_async_remote_copy(
                src_ref=gram_ref,
                dst_ref=arrived.at[k, position],
                send_sem=g_send.at[k, 0],
                recv_sem=g_recv.at[k, position],
                device_id=peer(axis, shift, position),
                device_id_type=MESH,
            )

        for m in range(1, QUARTERS):
            exchange(mine ^ m, m).start()
        arrived[k, mine] = gram_ref[...]
        for m in range(1, QUARTERS):
            exchange(mine ^ m, m).wait_send()
        for m in range(1, QUARTERS):
            incoming(mine ^ m).wait_recv()
        total = arrived[k, 0]
        for position in range(1, QUARTERS):
            total = total + arrived[k, position]
        gram_ref[...] = total

    for p in range(2):
        for t, q, d in sends:
            link(p, t, q, d).wait_send()

        @pl.when(has_above)
        def _():
            side(p, 0, (grp + 1, me)).wait_send()

        @pl.when(has_below)
        def _():
            side(p, 1, (grp - 1, me)).wait_send()


def couple_both(hamiltonian, index, trial, weights):
    shard_blocks, nsrc, block_size, width = hamiltonian.shape
    states = trial.shape[2]
    cycle = lax.axis_size("blk")
    assert cycle == RING * RING
    groups = lax.axis_size("group")
    slab = pltpu.VMEM(trial.shape, jnp.bfloat16)
    flops = 4 * shard_blocks * nsrc * block_size * width * states
    result = jax.ShapeDtypeStruct((shard_blocks, block_size, states), jnp.float32)
    vmem = pl.BlockSpec(memory_space=pltpu.VMEM)
    return pl.pallas_call(
        functools.partial(coupling_kernel, groups, 1.0 / (shard_blocks * block_size * cycle * groups)),
        out_shape=(result, result, jax.ShapeDtypeStruct((states, states), jnp.float32)),
        in_specs=[pl.BlockSpec(memory_space=pltpu.SMEM), vmem, vmem, pl.BlockSpec(memory_space=pl.ANY)],
        out_specs=(vmem, vmem, vmem),
        scratch_shapes=[slab] * (2 * cycle + 2)
        + [
            slab,
            slab,
            pltpu.VMEM((2, shard_blocks, block_size, width), hamiltonian.dtype),
            pltpu.SemaphoreType.DMA((2,)),
            pltpu.SemaphoreType.DMA((2, len(schedule()[1]))),
            pltpu.SemaphoreType.DMA((2, cycle, QUARTERS)),
            pltpu.SemaphoreType.DMA((2, 2)),
            pltpu.SemaphoreType.DMA((2, 2)),
            pltpu.VMEM((4, 4, states, states), jnp.float32),
            pltpu.SemaphoreType.DMA((4, 4)),
            pltpu.SemaphoreType.DMA((4, 4)),
        ],
        compiler_params=pltpu.CompilerParams(
            collective_id=0, has_side_effects=True, vmem_limit_bytes=48 * 1024 * 1024
        ),
        cost_estimate=pl.CostEstimate(
            flops=flops, transcendentals=0, bytes_accessed=hamiltonian.size * 4
        ),
    )(index, trial, weights, hamiltonian)


def gram_kernel(stages, gram_ref, out_ref, arrived, send_sem, recv_sem):
    place = {"group": lax.axis_index("group"), "blk": lax.axis_index("blk")}
    members = 4

    def field(axis, shift):
        return (place[axis] >> shift) % members

    def peer(axis, shift, position):
        other = dict(place)
        other[axis] = place[axis] + (position - field(axis, shift)) * (1 << shift)
        return (other["group"], other["blk"])

    barrier = pltpu.get_barrier_semaphore()
    for axis, shift in stages:
        for m in range(1, members):
            pl.semaphore_signal(
                barrier, inc=1, device_id=peer(axis, shift, field(axis, shift) ^ m), device_id_type=MESH
            )
    pl.semaphore_wait(barrier, len(stages) * (members - 1))
    out_ref[...] = gram_ref[...]
    for k, (axis, shift) in enumerate(stages):
        mine = field(axis, shift)

        def exchange(position, m):
            return pltpu.make_async_remote_copy(
                src_ref=out_ref,
                dst_ref=arrived.at[k, mine],
                send_sem=send_sem.at[k, m],
                recv_sem=recv_sem.at[k, mine],
                device_id=peer(axis, shift, position),
                device_id_type=MESH,
            )

        def incoming(position):
            return pltpu.make_async_remote_copy(
                src_ref=out_ref,
                dst_ref=arrived.at[k, position],
                send_sem=send_sem.at[k, 0],
                recv_sem=recv_sem.at[k, position],
                device_id=peer(axis, shift, position),
                device_id_type=MESH,
            )

        for m in range(1, members):
            exchange(mine ^ m, m).start()
        arrived[k, mine] = out_ref[...]
        for m in range(1, members):
            exchange(mine ^ m, m).wait_send()
        for m in range(1, members):
            incoming(mine ^ m).wait_recv()
        total = arrived[k, 0]
        for position in range(1, members):
            total = total + arrived[k, position]
        out_ref[...] = total


def summed_over_mesh(value):
    stages = []
    for axis in ("blk", "group"):
        size = lax.axis_size(axis)
        assert size == 16
        stages += [(axis, 0), (axis, 2)]
    return pl.pallas_call(
        functools.partial(gram_kernel, stages),
        out_shape=jax.ShapeDtypeStruct(value.shape, value.dtype),
        in_specs=[pl.BlockSpec(memory_space=pltpu.VMEM)],
        out_specs=pl.BlockSpec(memory_space=pltpu.VMEM),
        scratch_shapes=[
            pltpu.VMEM((len(stages), 4) + value.shape, value.dtype),
            pltpu.SemaphoreType.DMA((len(stages), 4)),
            pltpu.SemaphoreType.DMA((len(stages), 4)),
        ],
        compiler_params=pltpu.CompilerParams(collective_id=1, has_side_effects=True),
    )(value)


def on_device(hamiltonian, block_columns, potential, trial_slab):
    shard_blocks = hamiltonian.shape[0]
    block_size = hamiltonian.shape[2]
    states = trial_slab.shape[1]
    index = jnp.transpose(block_columns, (0, 2, 1)).reshape(-1)
    start_slab = trial_slab.reshape(shard_blocks, block_size, states)
    weights = potential.reshape(shard_blocks, block_size, 1)
    filtered_once, filtered, gram = couple_both(hamiltonian, index, start_slab, weights)
    flat = filtered.reshape(shard_blocks * block_size, states)
    lower = lax.linalg.cholesky(gram, symmetrize_input=False)
    ortho_slab = lax.linalg.triangular_solve(
        lower, flat, left_side=False, lower=True, transpose_a=True
    )
    return (ortho_slab, jnp.transpose(lower))


def solution(mesh):
    placed = (
        P(("group", "blk"), None, None, None),
        P(("group", "blk"), None, None),
        P(("group", "blk")),
        P(("group", "blk"), None),
    )
    return jax.shard_map(
        on_device,
        mesh=mesh,
        in_specs=placed,
        out_specs=(P(("group", "blk"), None), P()),
        check_vma=False,
    )
```

```python
import functools

import jax
import jax.numpy as jnp
from jax import lax
from jax.experimental import pallas as pl
from jax.experimental.pallas import tpu as pltpu
from jax.sharding import PartitionSpec as P

precise = lax.Precision.HIGHEST
MESH = pl.DeviceIdType.MESH


RING = 4
QUARTERS = 4
NEIGHBOURS = (1, 3, 4, 12)


def forwards(t, q):
    tx, ty = t & 3, t >> 2
    out = []
    if q < 2:
        if t == 0:
            out += [1, 3]
        if ty == 0 and tx == 1 and q == 0:
            out.append(3)
        if ty == 0 and tx == 3 and q == 1:
            out.append(1)
        if ty == 0:
            out += [4, 12]
        if ty == 1 and q == 0:
            out.append(12)
        if ty == 3 and q == 1:
            out.append(4)
    else:
        if t == 0:
            out += [4, 12]
        if tx == 0 and ty == 1 and q == 2:
            out.append(12)
        if tx == 0 and ty == 3 and q == 3:
            out.append(4)
        if tx == 0:
            out += [1, 3]
        if tx == 1 and q == 2:
            out.append(3)
        if tx == 3 and q == 3:
            out.append(1)
    return out


def schedule():
    level = {(0, q): 0 for q in range(QUARTERS)}
    sends = []
    frontier = [(0, q) for q in range(QUARTERS)]
    while frontier:
        nxt = []
        for t, q in frontier:
            for d in forwards(t, q):
                dest = (t ^ d, q)
                assert dest not in level
                level[dest] = level[(t, q)] + 1
                sends.append((t, q, d))
                nxt.append(dest)
        frontier = nxt
    assert len(level) == RING * RING * QUARTERS
    return level, sends


def coupling_kernel(groups, scale, index_ref, trial_ref, weight_ref, ham_hbm, once_ref, next_ref, gram_ref, *scratch):
    cycle = RING * RING
    held_sets = (scratch[: cycle + 1], scratch[cycle + 1 : 2 * cycle + 2])
    start_ref, rounded, ham_buf, ham_sem, send_sem, recv_sem, side_send, side_recv, arrived, g_send, g_recv = scratch[2 * cycle + 2 :]
    shard_blocks, nsrc, block_size, width = ham_hbm.shape
    per_source = width // block_size
    part = shard_blocks // QUARTERS
    me = lax.axis_index("blk")
    grp = lax.axis_index("group")
    has_below = grp > 0
    has_above = grp < groups - 1
    level, sends = schedule()
    send_index = {item: k for k, item in enumerate(sends)}
    owns = (start_ref, rounded)
    outs = (once_ref, next_ref)

    def buf(p, t):
        return owns[p] if t == 0 else held_sets[p][t - 1]

    def quarter(ref, q):
        return ref.at[pl.ds(q * part, part)]

    def link(p, t, q, d):
        return pltpu.make_async_remote_copy(
            src_ref=quarter(buf(p, t), q),
            dst_ref=quarter(buf(p, t ^ d), q),
            send_sem=send_sem.at[p, send_index[(t, q, d)]],
            recv_sem=recv_sem.at[p, t ^ d, q],
            device_id=(grp, me ^ d),
            device_id_type=MESH,
        )

    def arrival(p, t, q):
        return pltpu.make_async_remote_copy(
            src_ref=quarter(owns[p], q),
            dst_ref=quarter(buf(p, t), q),
            send_sem=side_send.at[p, 0],
            recv_sem=recv_sem.at[p, t, q],
            device_id=(grp, me),
            device_id_type=MESH,
        )

    def side(p, k, device):
        dst = held_sets[p][cycle - 1 + k]
        return pltpu.make_async_remote_copy(
            src_ref=owns[p],
            dst_ref=dst,
            send_sem=side_send.at[p, k],
            recv_sem=side_recv.at[p, k],
            device_id=device,
            device_id_type=MESH,
        )

    start_ref[...] = trial_ref[...].astype(start_ref.dtype)
    barrier = pltpu.get_barrier_semaphore()
    for d in NEIGHBOURS:
        pl.semaphore_signal(barrier, inc=1, device_id=(grp, me ^ d), device_id_type=MESH)

    @pl.when(has_below)
    def _():
        pl.semaphore_signal(barrier, inc=1, device_id=(grp - 1, me), device_id_type=MESH)

    @pl.when(has_above)
    def _():
        pl.semaphore_signal(barrier, inc=1, device_id=(grp + 1, me), device_id_type=MESH)

    place = {"group": grp, "blk": me}
    stages = [("blk", 0), ("blk", 2), ("group", 0), ("group", 2)]

    def field(axis, shift):
        return (place[axis] >> shift) % QUARTERS

    def peer(axis, shift, position):
        other = dict(place)
        other[axis] = place[axis] + (position - field(axis, shift)) * (1 << shift)
        return (other["group"], other["blk"])

    for axis, shift in stages:
        for m in range(1, QUARTERS):
            pl.semaphore_signal(
                barrier, inc=1, device_id=peer(axis, shift, field(axis, shift) ^ m), device_id_type=MESH
            )
    expected = len(NEIGHBOURS) + has_below.astype(jnp.int32) + has_above.astype(jnp.int32)
    pl.semaphore_wait(barrier, expected + len(stages) * (QUARTERS - 1))

    def send_own(p):
        for t, q, d in sends:
            if t == 0:
                link(p, t, q, d).start()

        @pl.when(has_above)
        def _():
            side(p, 0, (grp + 1, me)).start()

        @pl.when(has_below)
        def _():
            side(p, 1, (grp - 1, me)).start()

    top = max(level.values())
    steps = []
    for p in range(2):
        steps += [(p, "send", 0), (p, "own", 0), (p, "below", nsrc - 2), (p, "above", nsrc - 1)]
        for lv in range(1, top + 1):
            ready = [t for t in range(1, cycle) if max(level[(t, q)] for q in range(QUARTERS)) == lv]
            steps.append((p, "arrive", lv))
            steps += [(p, "slot", t) for t in ready]
        steps.append((p, "finish", 0))

    compute_steps = [x for x in steps if x[1] in ("own", "below", "above", "slot")]

    def source_of(kind, t):
        if kind == "own":
            return me
        if kind == "slot":
            return me ^ t
        return t

    def ham_copy(i, slot):
        p, kind, t = compute_steps[i]
        return pltpu.make_async_copy(
            ham_hbm.at[:, source_of(kind, t)], ham_buf.at[slot], ham_sem.at[slot]
        )

    once_ref[...] = jnp.zeros_like(once_ref)
    next_ref[...] = jnp.zeros_like(next_ref)
    ham_copy(0, 0).start()

    i = 0
    for p, kind, t in steps:
        if kind == "send":
            send_own(p)
            continue
        if kind == "arrive":
            for (slot_t, q), v in sorted(level.items()):
                if v == t:
                    arrival(p, slot_t, q).wait_recv()
                    for d in forwards(slot_t, q):
                        link(p, slot_t, q, d).start()
            continue
        if kind == "finish":
            if p == 0:
                once_ref[...] = 0.5 * (once_ref[...] + weight_ref[...] * trial_ref[...])
                rounded[...] = once_ref[...].astype(rounded.dtype)
            else:
                next_ref[...] = next_ref[...] + weight_ref[...] * once_ref[...] - trial_ref[...]
                local = jnp.zeros(gram_ref.shape, jnp.float32)
                for r in range(shard_blocks):
                    rows = next_ref[r]
                    local = local + jnp.dot(
                        rows.T, rows, precision=lax.Precision.HIGHEST, preferred_element_type=jnp.float32
                    )
                gram_ref[...] = local * scale
            continue
        slot = i % 2
        if kind == "own":
            data = owns[p]
        elif kind == "slot":
            data = buf(p, t)
        elif kind == "below":
            data = held_sets[p][cycle - 1]
        else:
            data = held_sets[p][cycle]
        source = source_of(kind, t)
        out_ref = outs[p]

        def work(data=data, source=source, slot=slot, kind=kind, p=p, out_ref=out_ref):
            if kind == "below":
                side(p, 0, (grp, me)).wait_recv()
            elif kind == "above":
                side(p, 1, (grp, me)).wait_recv()

            def row(r, carry):
                blocks = [data[index_ref[r, j, source]] for j in range(per_source)]
                picked = jnp.concatenate(blocks, axis=0)
                out_ref[r] += jnp.dot(
                    ham_buf[slot, r], picked, preferred_element_type=jnp.float32
                )
                return carry

            lax.fori_loop(0, shard_blocks, row, 0, unroll=True)

        ham_copy(i, slot).wait()
        if i + 1 < len(compute_steps):
            ham_copy(i + 1, 1 - slot).start()
        if kind == "below":
            pl.when(has_below)(work)
        elif kind == "above":
            pl.when(has_above)(work)
        else:
            work()
        i += 1

    for k, (axis, shift) in enumerate(stages):
        mine = field(axis, shift)

        def exchange(position, m):
            return pltpu.make_async_remote_copy(
                src_ref=gram_ref,
                dst_ref=arrived.at[k, mine],
                send_sem=g_send.at[k, m],
                recv_sem=g_recv.at[k, mine],
                device_id=peer(axis, shift, position),
                device_id_type=MESH,
            )

        def incoming(position):
            return pltpu.make_async_remote_copy(
                src_ref=gram_ref,
                dst_ref=arrived.at[k, position],
                send_sem=g_send.at[k, 0],
                recv_sem=g_recv.at[k, position],
                device_id=peer(axis, shift, position),
                device_id_type=MESH,
            )

        for m in range(1, QUARTERS):
            exchange(mine ^ m, m).start()
        arrived[k, mine] = gram_ref[...]
        for m in range(1, QUARTERS):
            exchange(mine ^ m, m).wait_send()
        for m in range(1, QUARTERS):
            incoming(mine ^ m).wait_recv()
        total = arrived[k, 0]
        for position in range(1, QUARTERS):
            total = total + arrived[k, position]
        gram_ref[...] = total

    for p in range(2):
        for t, q, d in sends:
            link(p, t, q, d).wait_send()

        @pl.when(has_above)
        def _():
            side(p, 0, (grp + 1, me)).wait_send()

        @pl.when(has_below)
        def _():
            side(p, 1, (grp - 1, me)).wait_send()


def couple_both(hamiltonian, index, trial, weights):
    shard_blocks, nsrc, block_size, width = hamiltonian.shape
    states = trial.shape[2]
    cycle = lax.axis_size("blk")
    assert cycle == RING * RING
    groups = lax.axis_size("group")
    slab = pltpu.VMEM(trial.shape, jnp.bfloat16)
    flops = 4 * shard_blocks * nsrc * block_size * width * states
    result = jax.ShapeDtypeStruct((shard_blocks, block_size, states), jnp.float32)
    vmem = pl.BlockSpec(memory_space=pltpu.VMEM)
    return pl.pallas_call(
        functools.partial(coupling_kernel, groups, 1.0 / (shard_blocks * block_size * cycle * groups)),
        out_shape=(result, result, jax.ShapeDtypeStruct((states, states), jnp.float32)),
        in_specs=[pl.BlockSpec(memory_space=pltpu.SMEM), vmem, vmem, pl.BlockSpec(memory_space=pl.ANY)],
        out_specs=(vmem, vmem, vmem),
        scratch_shapes=[slab] * (2 * cycle + 2)
        + [
            slab,
            slab,
            pltpu.VMEM((2, shard_blocks, block_size, width), hamiltonian.dtype),
            pltpu.SemaphoreType.DMA((2,)),
            pltpu.SemaphoreType.DMA((2, len(schedule()[1]))),
            pltpu.SemaphoreType.DMA((2, cycle, QUARTERS)),
            pltpu.SemaphoreType.DMA((2, 2)),
            pltpu.SemaphoreType.DMA((2, 2)),
            pltpu.VMEM((4, 4, states, states), jnp.float32),
            pltpu.SemaphoreType.DMA((4, 4)),
            pltpu.SemaphoreType.DMA((4, 4)),
        ],
        compiler_params=pltpu.CompilerParams(
            collective_id=0, has_side_effects=True, vmem_limit_bytes=48 * 1024 * 1024
        ),
        cost_estimate=pl.CostEstimate(
            flops=flops, transcendentals=0, bytes_accessed=hamiltonian.size * 4
        ),
    )(index, trial, weights, hamiltonian)


def gram_kernel(stages, gram_ref, out_ref, arrived, send_sem, recv_sem):
    place = {"group": lax.axis_index("group"), "blk": lax.axis_index("blk")}
    members = 4

    def field(axis, shift):
        return (place[axis] >> shift) % members

    def peer(axis, shift, position):
        other = dict(place)
        other[axis] = place[axis] + (position - field(axis, shift)) * (1 << shift)
        return (other["group"], other["blk"])

    barrier = pltpu.get_barrier_semaphore()
    for axis, shift in stages:
        for m in range(1, members):
            pl.semaphore_signal(
                barrier, inc=1, device_id=peer(axis, shift, field(axis, shift) ^ m), device_id_type=MESH
            )
    pl.semaphore_wait(barrier, len(stages) * (members - 1))
    out_ref[...] = gram_ref[...]
    for k, (axis, shift) in enumerate(stages):
        mine = field(axis, shift)

        def exchange(position, m):
            return pltpu.make_async_remote_copy(
                src_ref=out_ref,
                dst_ref=arrived.at[k, mine],
                send_sem=send_sem.at[k, m],
                recv_sem=recv_sem.at[k, mine],
                device_id=peer(axis, shift, position),
                device_id_type=MESH,
            )

        def incoming(position):
            return pltpu.make_async_remote_copy(
                src_ref=out_ref,
                dst_ref=arrived.at[k, position],
                send_sem=send_sem.at[k, 0],
                recv_sem=recv_sem.at[k, position],
                device_id=peer(axis, shift, position),
                device_id_type=MESH,
            )

        for m in range(1, members):
            exchange(mine ^ m, m).start()
        arrived[k, mine] = out_ref[...]
        for m in range(1, members):
            exchange(mine ^ m, m).wait_send()
        for m in range(1, members):
            incoming(mine ^ m).wait_recv()
        total = arrived[k, 0]
        for position in range(1, members):
            total = total + arrived[k, position]
        out_ref[...] = total


def summed_over_mesh(value):
    stages = []
    for axis in ("blk", "group"):
        size = lax.axis_size(axis)
        assert size == 16
        stages += [(axis, 0), (axis, 2)]
    return pl.pallas_call(
        functools.partial(gram_kernel, stages),
        out_shape=jax.ShapeDtypeStruct(value.shape, value.dtype),
        in_specs=[pl.BlockSpec(memory_space=pltpu.VMEM)],
        out_specs=pl.BlockSpec(memory_space=pltpu.VMEM),
        scratch_shapes=[
            pltpu.VMEM((len(stages), 4) + value.shape, value.dtype),
            pltpu.SemaphoreType.DMA((len(stages), 4)),
            pltpu.SemaphoreType.DMA((len(stages), 4)),
        ],
        compiler_params=pltpu.CompilerParams(collective_id=1, has_side_effects=True),
    )(value)


def on_device(hamiltonian, block_columns, potential, trial_slab):
    shard_blocks = hamiltonian.shape[0]
    block_size = hamiltonian.shape[2]
    states = trial_slab.shape[1]
    index = jnp.transpose(block_columns, (0, 2, 1))
    start_slab = trial_slab.reshape(shard_blocks, block_size, states)
    weights = potential.reshape(shard_blocks, block_size, 1)
    filtered_once, filtered, gram = couple_both(hamiltonian, index, start_slab, weights)
    flat = filtered.reshape(shard_blocks * block_size, states)
    lower = lax.linalg.cholesky(gram, symmetrize_input=False)
    ortho_slab = lax.linalg.triangular_solve(
        lower, flat, left_side=False, lower=True, transpose_a=True
    )
    return (ortho_slab, jnp.transpose(lower))


def solution(mesh):
    placed = (
        P(("group", "blk"), None, None, None),
        P(("group", "blk"), None, None),
        P(("group", "blk")),
        P(("group", "blk"), None),
    )
    return jax.shard_map(
        on_device,
        mesh=mesh,
        in_specs=placed,
        out_specs=(P(("group", "blk"), None), P()),
        check_vma=False,
    )
```

```python
import functools

import jax
import jax.numpy as jnp
from jax import lax
from jax.experimental import pallas as pl
from jax.experimental.pallas import tpu as pltpu
from jax.sharding import PartitionSpec as P

precise = lax.Precision.HIGHEST
MESH = pl.DeviceIdType.MESH


RING = 4
QUARTERS = 4
NEIGHBOURS = (1, 3, 4, 12)


def forwards(t, q):
    tx, ty = t & 3, t >> 2
    out = []
    if q < 2:
        if t == 0:
            out += [1, 3]
        if ty == 0 and tx == 1 and q == 0:
            out.append(3)
        if ty == 0 and tx == 3 and q == 1:
            out.append(1)
        if ty == 0:
            out += [4, 12]
        if ty == 1 and q == 0:
            out.append(12)
        if ty == 3 and q == 1:
            out.append(4)
    else:
        if t == 0:
            out += [4, 12]
        if tx == 0 and ty == 1 and q == 2:
            out.append(12)
        if tx == 0 and ty == 3 and q == 3:
            out.append(4)
        if tx == 0:
            out += [1, 3]
        if tx == 1 and q == 2:
            out.append(3)
        if tx == 3 and q == 3:
            out.append(1)
    return out


def schedule():
    level = {(0, q): 0 for q in range(QUARTERS)}
    sends = []
    frontier = [(0, q) for q in range(QUARTERS)]
    while frontier:
        nxt = []
        for t, q in frontier:
            for d in forwards(t, q):
                dest = (t ^ d, q)
                assert dest not in level
                level[dest] = level[(t, q)] + 1
                sends.append((t, q, d))
                nxt.append(dest)
        frontier = nxt
    assert len(level) == RING * RING * QUARTERS
    return level, sends


def coupling_kernel(groups, scale, index_ref, trial_ref, weight_ref, ham_hbm, once_ref, next_ref, gram_ref, *scratch):
    cycle = RING * RING
    held_sets = (scratch[: cycle + 1], scratch[cycle + 1 : 2 * cycle + 2])
    start_ref, rounded, ham_buf, ham_sem, send_sem, recv_sem, side_send, side_recv, arrived, g_send, g_recv = scratch[2 * cycle + 2 :]
    shard_blocks, nsrc, block_size, width = ham_hbm.shape
    per_source = width // block_size
    part = shard_blocks // QUARTERS
    me = lax.axis_index("blk")
    grp = lax.axis_index("group")
    has_below = grp > 0
    has_above = grp < groups - 1
    level, sends = schedule()
    send_index = {item: k for k, item in enumerate(sends)}
    owns = (start_ref, rounded)
    outs = (once_ref, next_ref)

    def buf(p, t):
        return owns[p] if t == 0 else held_sets[p][t - 1]

    def quarter(ref, q):
        return ref.at[pl.ds(q * part, part)]

    def link(p, t, q, d):
        return pltpu.make_async_remote_copy(
            src_ref=quarter(buf(p, t), q),
            dst_ref=quarter(buf(p, t ^ d), q),
            send_sem=send_sem.at[p, send_index[(t, q, d)]],
            recv_sem=recv_sem.at[p, t ^ d, q],
            device_id=(grp, me ^ d),
            device_id_type=MESH,
        )

    def arrival(p, t, q):
        return pltpu.make_async_remote_copy(
            src_ref=quarter(owns[p], q),
            dst_ref=quarter(buf(p, t), q),
            send_sem=side_send.at[p, 0],
            recv_sem=recv_sem.at[p, t, q],
            device_id=(grp, me),
            device_id_type=MESH,
        )

    def side(p, k, device):
        dst = held_sets[p][cycle - 1 + k]
        return pltpu.make_async_remote_copy(
            src_ref=owns[p],
            dst_ref=dst,
            send_sem=side_send.at[p, k],
            recv_sem=side_recv.at[p, k],
            device_id=device,
            device_id_type=MESH,
        )

    start_ref[...] = trial_ref[...].astype(start_ref.dtype)
    barrier = pltpu.get_barrier_semaphore()
    for d in NEIGHBOURS:
        pl.semaphore_signal(barrier, inc=1, device_id=(grp, me ^ d), device_id_type=MESH)

    @pl.when(has_below)
    def _():
        pl.semaphore_signal(barrier, inc=1, device_id=(grp - 1, me), device_id_type=MESH)

    @pl.when(has_above)
    def _():
        pl.semaphore_signal(barrier, inc=1, device_id=(grp + 1, me), device_id_type=MESH)

    place = {"group": grp, "blk": me}
    stages = [("blk", 0), ("blk", 2), ("group", 0), ("group", 2)]

    def field(axis, shift):
        return (place[axis] >> shift) % QUARTERS

    def peer(axis, shift, position):
        other = dict(place)
        other[axis] = place[axis] + (position - field(axis, shift)) * (1 << shift)
        return (other["group"], other["blk"])

    for axis, shift in stages:
        for m in range(1, QUARTERS):
            pl.semaphore_signal(
                barrier, inc=1, device_id=peer(axis, shift, field(axis, shift) ^ m), device_id_type=MESH
            )
    expected = len(NEIGHBOURS) + has_below.astype(jnp.int32) + has_above.astype(jnp.int32)
    pl.semaphore_wait(barrier, expected + len(stages) * (QUARTERS - 1))

    def send_own(p):
        for t, q, d in sends:
            if t == 0:
                link(p, t, q, d).start()

        @pl.when(has_above)
        def _():
            side(p, 0, (grp + 1, me)).start()

        @pl.when(has_below)
        def _():
            side(p, 1, (grp - 1, me)).start()

    top = max(level.values())
    steps = []
    for p in range(2):
        steps += [(p, "send", 0), (p, "own", 0), (p, "below", nsrc - 2), (p, "above", nsrc - 1)]
        for lv in range(1, top + 1):
            ready = [t for t in range(1, cycle) if max(level[(t, q)] for q in range(QUARTERS)) == lv]
            steps.append((p, "arrive", lv))
            steps += [(p, "slot", t) for t in ready]
        steps.append((p, "finish", 0))

    compute_steps = [x for x in steps if x[1] in ("own", "below", "above", "slot")]

    def source_of(kind, t):
        if kind == "own":
            return me
        if kind == "slot":
            return me ^ t
        return t

    def ham_copy(i, slot):
        p, kind, t = compute_steps[i]
        return pltpu.make_async_copy(
            ham_hbm.at[:, source_of(kind, t)], ham_buf.at[slot], ham_sem.at[slot]
        )

    once_ref[...] = jnp.zeros_like(once_ref)
    next_ref[...] = jnp.zeros_like(next_ref)
    ham_copy(0, 0).start()

    i = 0
    for p, kind, t in steps:
        if kind == "send":
            send_own(p)
            continue
        if kind == "arrive":
            for (slot_t, q), v in sorted(level.items()):
                if v == t:
                    arrival(p, slot_t, q).wait_recv()
                    for d in forwards(slot_t, q):
                        link(p, slot_t, q, d).start()
            continue
        if kind == "finish":
            if p == 0:
                columns = jnp.transpose(weight_ref[...])
                rows_per = columns.shape[0] // (shard_blocks // columns.shape[1])
                weight_col = [
                    columns[(b % (columns.shape[0] // rows_per)) * rows_per : (b % (columns.shape[0] // rows_per) + 1) * rows_per,
                            b // (columns.shape[0] // rows_per) : b // (columns.shape[0] // rows_per) + 1]
                    for b in range(shard_blocks)
                ]
                for b in range(shard_blocks):
                    once_ref[b] = 0.5 * (once_ref[b] + weight_col[b] * trial_ref[b])
                rounded[...] = once_ref[...].astype(rounded.dtype)
            else:
                for b in range(shard_blocks):
                    next_ref[b] = next_ref[b] + weight_col[b] * once_ref[b] - trial_ref[b]
                local = jnp.zeros(gram_ref.shape, jnp.float32)
                for r in range(shard_blocks):
                    rows = next_ref[r]
                    local = local + jnp.dot(
                        rows.T, rows, precision=lax.Precision.HIGHEST, preferred_element_type=jnp.float32
                    )
                gram_ref[...] = local * scale
            continue
        slot = i % 2
        if kind == "own":
            data = owns[p]
        elif kind == "slot":
            data = buf(p, t)
        elif kind == "below":
            data = held_sets[p][cycle - 1]
        else:
            data = held_sets[p][cycle]
        source = source_of(kind, t)
        out_ref = outs[p]

        def work(data=data, source=source, slot=slot, kind=kind, p=p, out_ref=out_ref):
            if kind == "below":
                side(p, 0, (grp, me)).wait_recv()
            elif kind == "above":
                side(p, 1, (grp, me)).wait_recv()

            def row(r, carry):
                blocks = [data[index_ref[(r * per_source + j) * nsrc + source]] for j in range(per_source)]
                picked = jnp.concatenate(blocks, axis=0)
                out_ref[r] += jnp.dot(
                    ham_buf[slot, r], picked, preferred_element_type=jnp.float32
                )
                return carry

            lax.fori_loop(0, shard_blocks, row, 0, unroll=True)

        ham_copy(i, slot).wait()
        if i + 1 < len(compute_steps):
            ham_copy(i + 1, 1 - slot).start()
        if kind == "below":
            pl.when(has_below)(work)
        elif kind == "above":
            pl.when(has_above)(work)
        else:
            work()
        i += 1

    for k, (axis, shift) in enumerate(stages):
        mine = field(axis, shift)

        def exchange(position, m):
            return pltpu.make_async_remote_copy(
                src_ref=gram_ref,
                dst_ref=arrived.at[k, mine],
                send_sem=g_send.at[k, m],
                recv_sem=g_recv.at[k, mine],
                device_id=peer(axis, shift, position),
                device_id_type=MESH,
            )

        def incoming(position):
            return pltpu.make_async_remote_copy(
                src_ref=gram_ref,
                dst_ref=arrived.at[k, position],
                send_sem=g_send.at[k, 0],
                recv_sem=g_recv.at[k, position],
                device_id=peer(axis, shift, position),
                device_id_type=MESH,
            )

        for m in range(1, QUARTERS):
            exchange(mine ^ m, m).start()
        arrived[k, mine] = gram_ref[...]
        for m in range(1, QUARTERS):
            exchange(mine ^ m, m).wait_send()
        for m in range(1, QUARTERS):
            incoming(mine ^ m).wait_recv()
        total = arrived[k, 0]
        for position in range(1, QUARTERS):
            total = total + arrived[k, position]
        gram_ref[...] = total

    for p in range(2):
        for t, q, d in sends:
            link(p, t, q, d).wait_send()

        @pl.when(has_above)
        def _():
            side(p, 0, (grp + 1, me)).wait_send()

        @pl.when(has_below)
        def _():
            side(p, 1, (grp - 1, me)).wait_send()


def couple_both(hamiltonian, index, trial, weights):
    shard_blocks, nsrc, block_size, width = hamiltonian.shape
    states = trial.shape[2]
    cycle = lax.axis_size("blk")
    assert cycle == RING * RING
    groups = lax.axis_size("group")
    slab = pltpu.VMEM(trial.shape, jnp.bfloat16)
    flops = 4 * shard_blocks * nsrc * block_size * width * states
    result = jax.ShapeDtypeStruct((shard_blocks, block_size, states), jnp.float32)
    vmem = pl.BlockSpec(memory_space=pltpu.VMEM)
    return pl.pallas_call(
        functools.partial(coupling_kernel, groups, 1.0 / (shard_blocks * block_size * cycle * groups)),
        out_shape=(result, result, jax.ShapeDtypeStruct((states, states), jnp.float32)),
        in_specs=[pl.BlockSpec(memory_space=pltpu.SMEM), vmem, vmem, pl.BlockSpec(memory_space=pl.ANY)],
        out_specs=(vmem, vmem, vmem),
        scratch_shapes=[slab] * (2 * cycle + 2)
        + [
            slab,
            slab,
            pltpu.VMEM((2, shard_blocks, block_size, width), hamiltonian.dtype),
            pltpu.SemaphoreType.DMA((2,)),
            pltpu.SemaphoreType.DMA((2, len(schedule()[1]))),
            pltpu.SemaphoreType.DMA((2, cycle, QUARTERS)),
            pltpu.SemaphoreType.DMA((2, 2)),
            pltpu.SemaphoreType.DMA((2, 2)),
            pltpu.VMEM((4, 4, states, states), jnp.float32),
            pltpu.SemaphoreType.DMA((4, 4)),
            pltpu.SemaphoreType.DMA((4, 4)),
        ],
        compiler_params=pltpu.CompilerParams(
            collective_id=0, has_side_effects=True, vmem_limit_bytes=48 * 1024 * 1024
        ),
        cost_estimate=pl.CostEstimate(
            flops=flops, transcendentals=0, bytes_accessed=hamiltonian.size * 4
        ),
    )(index, trial, weights, hamiltonian)


def gram_kernel(stages, gram_ref, out_ref, arrived, send_sem, recv_sem):
    place = {"group": lax.axis_index("group"), "blk": lax.axis_index("blk")}
    members = 4

    def field(axis, shift):
        return (place[axis] >> shift) % members

    def peer(axis, shift, position):
        other = dict(place)
        other[axis] = place[axis] + (position - field(axis, shift)) * (1 << shift)
        return (other["group"], other["blk"])

    barrier = pltpu.get_barrier_semaphore()
    for axis, shift in stages:
        for m in range(1, members):
            pl.semaphore_signal(
                barrier, inc=1, device_id=peer(axis, shift, field(axis, shift) ^ m), device_id_type=MESH
            )
    pl.semaphore_wait(barrier, len(stages) * (members - 1))
    out_ref[...] = gram_ref[...]
    for k, (axis, shift) in enumerate(stages):
        mine = field(axis, shift)

        def exchange(position, m):
            return pltpu.make_async_remote_copy(
                src_ref=out_ref,
                dst_ref=arrived.at[k, mine],
                send_sem=send_sem.at[k, m],
                recv_sem=recv_sem.at[k, mine],
                device_id=peer(axis, shift, position),
                device_id_type=MESH,
            )

        def incoming(position):
            return pltpu.make_async_remote_copy(
                src_ref=out_ref,
                dst_ref=arrived.at[k, position],
                send_sem=send_sem.at[k, 0],
                recv_sem=recv_sem.at[k, position],
                device_id=peer(axis, shift, position),
                device_id_type=MESH,
            )

        for m in range(1, members):
            exchange(mine ^ m, m).start()
        arrived[k, mine] = out_ref[...]
        for m in range(1, members):
            exchange(mine ^ m, m).wait_send()
        for m in range(1, members):
            incoming(mine ^ m).wait_recv()
        total = arrived[k, 0]
        for position in range(1, members):
            total = total + arrived[k, position]
        out_ref[...] = total


def summed_over_mesh(value):
    stages = []
    for axis in ("blk", "group"):
        size = lax.axis_size(axis)
        assert size == 16
        stages += [(axis, 0), (axis, 2)]
    return pl.pallas_call(
        functools.partial(gram_kernel, stages),
        out_shape=jax.ShapeDtypeStruct(value.shape, value.dtype),
        in_specs=[pl.BlockSpec(memory_space=pltpu.VMEM)],
        out_specs=pl.BlockSpec(memory_space=pltpu.VMEM),
        scratch_shapes=[
            pltpu.VMEM((len(stages), 4) + value.shape, value.dtype),
            pltpu.SemaphoreType.DMA((len(stages), 4)),
            pltpu.SemaphoreType.DMA((len(stages), 4)),
        ],
        compiler_params=pltpu.CompilerParams(collective_id=1, has_side_effects=True),
    )(value)


def on_device(hamiltonian, block_columns, potential, trial_slab):
    shard_blocks = hamiltonian.shape[0]
    block_size = hamiltonian.shape[2]
    states = trial_slab.shape[1]
    index = jnp.transpose(block_columns, (0, 2, 1)).reshape(-1)
    start_slab = trial_slab.reshape(shard_blocks, block_size, states)
    weights = potential.reshape(-1, 128)
    filtered_once, filtered, gram = couple_both(hamiltonian, index, start_slab, weights)
    flat = filtered.reshape(shard_blocks * block_size, states)
    lower = lax.linalg.cholesky(gram, symmetrize_input=False)
    ortho_slab = lax.linalg.triangular_solve(
        lower, flat, left_side=False, lower=True, transpose_a=True
    )
    return (ortho_slab, jnp.transpose(lower))


def solution(mesh):
    placed = (
        P(("group", "blk"), None, None, None),
        P(("group", "blk"), None, None),
        P(("group", "blk")),
        P(("group", "blk"), None),
    )
    return jax.shard_map(
        on_device,
        mesh=mesh,
        in_specs=placed,
        out_specs=(P(("group", "blk"), None), P()),
        check_vma=False,
    )
```
